128 devices in a mesh: gx: 8 (over z, core), gy: 16 (over y, x).
Axes of the slice: x: 4, y: 4, z: 4, core: 2. Of those that a mesh axis runs over, the one named last changes fastest.
Arguments:
- hidden: bfloat16 [8, 16384], replicated, may hold values from -6 to 6
- norm_gain: float32 [16384], replicated, may hold values from 0.5 to 1.5
- q_codes: int32 [16384, 8192], P('gx', 'gy'), may hold values from 0 to 255, as said below
- q_absmax: float32 [256, 16384], P('gx', 'gy'), may hold values from 0.0046875 to 0.046875
- kv_codes: int32 [16384, 1024], P('gx', 'gy'), may hold values from 0 to 255
- kv_absmax: float32 [256, 2048], P('gx', 'gy'), may hold values from 0.015625 to 0.15625
- o_codes: int32 [16384, 8192], P('gx', 'gy'), may hold values from 0 to 255, as said below
- o_absmax: float32 [256, 16384], P('gx', 'gy'), may hold values from 0.0046875 to 0.046875
- q_down: bfloat16 [8, 16384, 16], P(None, 'gx'), may hold values from -0.140625 to 0.140625
- q_up: bfloat16 [8, 16, 16384], P(None, None, 'gy'), may hold values from -1.5 to 1.5
- q_magnitude: float32 [8, 16384], P(None, 'gy'), may hold values from 0.25 to 1.75
- o_down: bfloat16 [8, 16384, 16], P(None, 'gx'), may hold values from -0.140625 to 0.140625
- o_up: bfloat16 [8, 16, 16384], P(None, None, 'gy'), may hold values from -1.5 to 1.5
- o_magnitude: float32 [8, 16384], P(None, 'gy'), may hold values from 0.25 to 1.75
- tenant: int32 [8], replicated, may hold values from 0 to 7
- lengths: int32 [8], replicated, may hold values from 1 to 24576, as said below
- page_table: int32 [8, 96], replicated, may hold values from 0 to 639, as said below
- kv_cache: bfloat16 [640, 2, 256, 1024], P(('gx', 'gy')), may hold values from -1080 to 1080, as said below
Outputs:
- layer_out: bfloat16 [8, 16384], P('gx', 'gy')
The draws below stay inside these ranges and needn't reach their ends.
Inputs may be any that keep to these rules, and one draw needn't show every extreme that they name: `q_codes`: each word holds two 4-bit codes: word % 16 for the even column and word // 16 for the odd one. `kv_codes`: each word holds two 4-bit codes: word % 16 for the even column and word // 16 for the odd one. `o_codes`: each word holds two 4-bit codes: word % 16 for the even column and word // 16 for the odd one. `lengths`: one row holds exactly 24576 tokens; every other row fewer than 16384. `page_table`: for j below ceil(lengths[r] / 256), entry [r, j] is the global slot of page j of row r: device index along gx+gy times 5 plus the slot on that device; no slot holds two pages; other entries are 0 and are not read. On every device the used slots are its first ones; no device holds more than 5 pages and some device holds exactly 5. `kv_cache`: row d * 5 + s holds slot s of device d; unused slots hold finite values.
All inputs are finite; a program needn't handle non-finite values.
Results may differ from the reference program's by a relative error of at most 0.01.
The reference program's roundings to bfloat16 on the way (of `normed`, `query` and `attended`) count: a program that leaves them out, or rounds other values in their place, can miss the bound.
Values may be sent and summed in bfloat16 or wider, within the bound.
A program may use at most 192 MiB of HBM per device.

```python
import math
import jax
import jax.numpy as jnp
from jax import lax

D = 16384
HEADS = 128
KV_HEADS = 8
HEAD_DIM = 128
RANK = 16
TENANTS = 8
QBLOCK = 64
PAGE = 256
MAXLEN = 24576
MEAN_LEN = 8192
ROWS = 8
QWIDTH = 16384
KVWIDTH = 2048
MAX_PAGES = 96
SLOTS = 5
ALL_SLOTS = 640
HOT = 8
N_GY = 16


def layout(key):
    root_key = jax.random.fold_in(key, 1234)
    pick_key, length_key, order_key = jax.random.split(root_key, 3)
    longest = jax.random.randint(pick_key, (), 0, ROWS)
    others = jax.random.randint(length_key, (ROWS,), 1, 2 * MEAN_LEN)
    row_lengths = jnp.where(jnp.arange(ROWS) == longest, MAXLEN, others).astype(jnp.int32)
    page_need = (row_lengths + PAGE - 1) // PAGE
    live_mask = jnp.arange(MAX_PAGES)[None, :] < page_need[:, None]
    live_rank = jnp.cumsum(live_mask.reshape(-1).astype(jnp.int32)) - 1
    device_total = ALL_SLOTS // SLOTS
    device_rank = jax.random.permutation(order_key, device_total)
    slot_ids = jnp.arange(ALL_SLOTS)
    device_of = slot_ids // SLOTS
    slot_of = slot_ids % SLOTS
    rank_of = device_rank[device_of]
    priority = jnp.where(rank_of < HOT, rank_of * SLOTS + slot_of, HOT * SLOTS + slot_of * device_total + rank_of)
    slot_order = jnp.argsort(priority, stable=True)
    chosen = slot_order[jnp.clip(live_rank, 0, ALL_SLOTS - 1)].reshape(ROWS, MAX_PAGES)
    table = jnp.where(live_mask, chosen, 0).astype(jnp.int32)
    return (row_lengths, table)


def draw_lengths(key, part):
    return layout(key)[0]


def draw_page_table(key, part):
    return layout(key)[1]


def draw_kv_cache(key, part):
    full_shape = (ALL_SLOTS, 2, PAGE, KV_HEADS * HEAD_DIM)
    normal_key = jax.random.fold_in(key, 99)
    values = jnp.clip(jax.random.normal(normal_key, full_shape, jnp.float32), -6.0, 6.0)
    is_key = jnp.arange(2)[None, :, None, None] == 0
    values = values * jnp.where(is_key, 2.5, 1.0)
    return values.astype(jnp.bfloat16)


def sign_matrix(key, sign_salt, row_count):
    return 2 * jax.random.randint(jax.random.fold_in(key, sign_salt), (TENANTS * RANK, row_count), 0, 2) - 1


def amplitude_level(key, sign_salt, row_count):
    offsets = jax.random.randint(jax.random.fold_in(key, sign_salt + 7), (2,), 0, 6)
    row_ids = jnp.arange(row_count)
    parity_low = ((row_ids + offsets[0]) % 2 == 0).astype(jnp.int32)
    third_low = ((row_ids + offsets[1]) % 3 == 0).astype(jnp.int32)
    return parity_low + third_low


def shrink_codes(codes, levels):
    return jnp.where(levels == 0, codes, jnp.where(levels == 1, 4 + codes // 2, 6 + codes // 4))


def signed_words(key, sign_salt, own_salt, row_count, word_count):
    signs = sign_matrix(key, sign_salt, row_count)
    group_of = jnp.arange(word_count) * (TENANTS * RANK) // word_count
    row_sign = jnp.take(signs, group_of, axis=0).T
    levels = amplitude_level(key, sign_salt, row_count)[:, None]
    drawn_words = jax.random.randint(jax.random.fold_in(key, own_salt), (row_count, word_count), 0, 65536)
    nibble_one = drawn_words % 16
    nibble_two = drawn_words // 16 % 16
    nibble_three = drawn_words // 256 % 16
    nibble_four = drawn_words // 4096
    low_code = jnp.where(row_sign > 0, jnp.maximum(nibble_one, nibble_two), jnp.minimum(nibble_one, nibble_two))
    high_code = jnp.where(row_sign > 0, jnp.maximum(nibble_three, nibble_four), jnp.minimum(nibble_three, nibble_four))
    low_code = shrink_codes(low_code, levels)
    high_code = shrink_codes(high_code, levels)
    return (low_code + 16 * high_code).astype(jnp.int32)


def drawn_down(key, sign_salt, own_salt, row_count):
    signs = sign_matrix(key, sign_salt, row_count).astype(jnp.float32).reshape(TENANTS, RANK, row_count)
    signs = jnp.transpose(signs, (0, 2, 1))
    noise_part = jnp.clip(jax.random.normal(jax.random.fold_in(key, own_salt), (TENANTS, row_count, RANK), jnp.float32), -6.0, 6.0)
    lean_size = jax.random.uniform(jax.random.fold_in(key, own_salt + 50), (TENANTS, 1, RANK), jnp.float32, 0.6, 1.2)
    lean_sign = (2 * jax.random.randint(jax.random.fold_in(key, own_salt + 51), (TENANTS, 1, RANK), 0, 2) - 1).astype(jnp.float32)
    position = jnp.arange(row_count, dtype=jnp.float32) / row_count
    row_factor = (10.0 ** (position - 0.5) / 1.47)[None, :, None]
    return ((noise_part + lean_size * lean_sign * signs) * row_factor * row_count ** (-0.5)).astype(jnp.bfloat16)


def draw_q_codes(key, part):
    return signed_words(key, 501, 601, D, QWIDTH // 2)


def draw_q_down(key, part):
    return drawn_down(key, 501, 602, D)


def draw_o_codes(key, part):
    return signed_words(key, 511, 611, QWIDTH, D // 2)


def draw_o_down(key, part):
    return drawn_down(key, 511, 612, QWIDTH)


def with_ends(drawn, stream_key, low, top_value):
    place = [jax.random.randint(jax.random.fold_in(stream_key, axis), (), 0, length) for axis, length in enumerate(drawn.shape)]
    main_axis = drawn.shape.index(max(drawn.shape))
    next_to = place[:main_axis] + [(place[main_axis] + 1) % drawn.shape[main_axis]] + place[main_axis + 1:]
    return drawn.at[tuple(place)].set(low).at[tuple(next_to)].set(top_value)


def steps_of(key, extent, cuts, smallest, high):
    def one(axis_at, shards_of):
        heights = jax.random.uniform(jax.random.fold_in(jax.random.fold_in(key, 6), axis_at), (shards_of,), jnp.float32, smallest / len(cuts), high / len(cuts))
        return jnp.repeat(jnp.exp(heights), extent[axis_at] // shards_of).reshape((-1,) + (1,) * (len(extent) - axis_at - 1))

    factor_of = one(*cuts[0])
    for cut in cuts[1:]:
        factor_of = factor_of * one(*cut)
    return factor_of


def bell_draw(rng, dims, scale, bound, shards=(), kind=jnp.bfloat16):
    drawn = jax.random.normal(rng, dims, jnp.float32) * scale
    if len(shards) > 0:
        drawn = steps_of(rng, dims, shards, -0.22, 0.18) * drawn
    return jnp.clip(drawn, min=-bound, max=bound).astype(kind)


def setup_inputs(seed: int = 0) -> dict:
    keys = jax.random.split(jax.random.key(seed), 19)
    return {
        "hidden": bell_draw(keys[0], (ROWS, D), 1.0, 6.0),
        "norm_gain": jnp.clip(1.0 + 0.1 * jax.random.normal(keys[1], (D,), jnp.float32), 0.5, 1.5),
        "q_codes": draw_q_codes(jax.random.fold_in(keys[18], 71), 0),
        "q_absmax": jnp.clip(jnp.exp(math.log(0.046875) - 2.3025851 * jax.random.uniform(keys[3], (D // QBLOCK, QWIDTH), jnp.float32) ** steps_of(keys[3], (D // QBLOCK, QWIDTH), ((0, 8), (1, 16)), -0.2, 0.2)), 0.0046875, 0.046875),
        "kv_codes": with_ends(jax.random.randint(keys[4], (D, KVWIDTH // 2), 0, 256), jax.random.fold_in(keys[4], 1), 0, 255).astype(jnp.int32),
        "kv_absmax": jnp.clip(jnp.exp(math.log(0.15625) - 2.3025851 * jax.random.uniform(keys[5], (D // QBLOCK, KVWIDTH), jnp.float32) ** steps_of(keys[5], (D // QBLOCK, KVWIDTH), ((0, 8), (1, 16)), -0.2, 0.2)), 0.015625, 0.15625),
        "o_codes": draw_o_codes(jax.random.fold_in(keys[18], 71), 0),
        "o_absmax": jnp.clip(jnp.exp(math.log(0.046875) - 2.3025851 * jax.random.uniform(keys[7], (QWIDTH // QBLOCK, D), jnp.float32) ** steps_of(keys[7], (QWIDTH // QBLOCK, D), ((0, 8), (1, 16)), -0.2, 0.2)), 0.0046875, 0.046875),
        "q_down": draw_q_down(jax.random.fold_in(keys[18], 71), 0),
        "q_up": bell_draw(keys[9], (TENANTS, RANK, QWIDTH), RANK ** -0.5, 1.5, ((2, 16),)),
        "q_magnitude": jnp.clip(1.0 + 0.15 * jax.random.normal(keys[10], (TENANTS, QWIDTH), jnp.float32), 0.25, 1.75),
        "o_down": draw_o_down(jax.random.fold_in(keys[18], 71), 0),
        "o_up": bell_draw(keys[12], (TENANTS, RANK, D), RANK ** -0.5, 1.5, ((2, 16),)),
        "o_magnitude": jnp.clip(1.0 + 0.15 * jax.random.normal(keys[13], (TENANTS, D), jnp.float32), 0.25, 1.75),
        "tenant": with_ends(jax.random.randint(keys[14], (ROWS,), 0, TENANTS), jax.random.fold_in(keys[14], 1), 0, TENANTS - 1).astype(jnp.int32),
        "lengths": draw_lengths(jax.random.fold_in(keys[18], 71), 0),
        "page_table": draw_page_table(jax.random.fold_in(keys[18], 71), 0),
        "kv_cache": draw_kv_cache(jax.random.fold_in(keys[18], 71), 0),
    }


NF4_LEVELS = (-1.0, -0.6961928009986877, -0.5250730514526367, -0.39491748809814453, -0.28444138169288635, -0.18477343022823334, -0.09105003625154495, 0.0, 0.07958029955625534, 0.16093020141124725, 0.24611230194568634, 0.33791524171829224, 0.44070982933044434, 0.5626170039176941, 0.7229568362236023, 1.0)
NORM_EPS = 1e-05
NEG_FILL = -1e+30
ROPE_BASE = 500000.0
PRECISE = lax.Precision.HIGHEST

def nf4_value(code_array):
    level_list = [jnp.float32(level_value) for level_value in NF4_LEVELS]
    for bit_place in range(4):
        bit_set = code_array // 2 ** bit_place % 2 == 1
        level_list = [jnp.where(bit_set, level_list[2 * pair_index + 1], level_list[2 * pair_index]) for pair_index in range(len(level_list) // 2)]
    return level_list[0]

def dequantize(packed, absmax):
    low_levels = nf4_value(packed % 16)
    high_levels = nf4_value(packed // 16)
    in_count, half_cols = packed.shape
    levels = jnp.stack([low_levels, high_levels], axis=-1).reshape(in_count // QBLOCK, QBLOCK, 2 * half_cols)
    return (levels * absmax[:, None, :]).reshape(in_count, 2 * half_cols).astype(jnp.bfloat16)

def rotate(values, positions):
    row_count = values.shape[0]
    half_dim = HEAD_DIM // 2
    frequency = ROPE_BASE ** (-2.0 * jnp.arange(half_dim, dtype=jnp.float32) / HEAD_DIM)
    angles = positions.astype(jnp.float32)[:, None, None] * frequency[None, None, :]
    cosine = jnp.cos(angles)
    sine_part = jnp.sin(angles)
    head_view = values.reshape(row_count, -1, HEAD_DIM)
    front_half = head_view[..., :half_dim]
    back_half = head_view[..., half_dim:]
    turned = jnp.concatenate([front_half * cosine - back_half * sine_part, back_half * cosine + front_half * sine_part], axis=-1)
    return turned.reshape(row_count, -1)

def weight_terms(inputs, down):
    down_float = down.astype(jnp.float32)

    def piece_terms(weight):
        weight_float = weight.astype(jnp.float32)
        product = jnp.dot(inputs, weight, preferred_element_type=jnp.float32)
        cross_terms = jnp.einsum('tdk,dc->tkc', down_float, weight_float, precision=PRECISE)
        squares = lax.optimization_barrier(jnp.sum(weight_float * weight_float, axis=0))
        return (product, cross_terms, squares)
    return piece_terms

def column_pieces(packed, absmax, piece_fn, piece_count):
    half_cols = packed.shape[1] // piece_count

    def one_piece(piece_index):
        codes_part = lax.dynamic_slice_in_dim(packed, piece_index * half_cols, half_cols, 1)
        absmax_part = lax.dynamic_slice_in_dim(absmax, piece_index * 2 * half_cols, 2 * half_cols, 1)
        return piece_fn(dequantize(codes_part, absmax_part))
    return lax.map(one_piece, jnp.arange(piece_count, dtype=jnp.int32))

def join_columns(stacked_part):
    moved = jnp.moveaxis(stacked_part, 0, -2)
    return moved.reshape(moved.shape[:-2] + (-1,))

def gram_terms(down):
    down_float = down.astype(jnp.float32)
    return jnp.einsum('tdk,tdl->tkl', down_float, down_float, precision=PRECISE)

def column_scale(cross_terms, squares, gram_matrix, up, magnitude):
    up_float = up.astype(jnp.float32)
    quadratic = jnp.einsum('tkc,tkl,tlc->tc', up_float, gram_matrix, up_float, precision=PRECISE)
    linear = lax.optimization_barrier(jnp.sum(up_float * cross_terms, axis=1))
    return magnitude.astype(jnp.float32) * lax.rsqrt(squares[None, :] + 2.0 * linear + quadratic)

def adapter_term(inputs, down, up, onehot):
    middle = jnp.einsum('rd,tdk->rtk', inputs.astype(jnp.float32), down.astype(jnp.float32), precision=PRECISE) * onehot[:, :, None]
    return jnp.dot(middle.reshape(middle.shape[0], -1), up.astype(jnp.float32).reshape(-1, up.shape[2]), precision=PRECISE)

def reference(hidden, norm_gain, q_codes, q_absmax, kv_codes, kv_absmax, o_codes, o_absmax, q_down, q_up, q_magnitude, o_down, o_up, o_magnitude, tenant, lengths, page_table, kv_cache):
    states = hidden.astype(jnp.float32)
    mean_square = lax.optimization_barrier(jnp.mean(states * states, axis=1, keepdims=True))
    normed = (states * lax.rsqrt(mean_square + NORM_EPS) * norm_gain.astype(jnp.float32)[None, :]).astype(jnp.bfloat16)
    onehot = (tenant[:, None] == jnp.arange(TENANTS, dtype=jnp.int32)[None, :]).astype(jnp.float32)
    q_parts = column_pieces(q_codes, q_absmax, weight_terms(normed, q_down), N_GY)
    query_base, q_cross, q_squares = [join_columns(stacked_part) for stacked_part in q_parts]
    q_scale = column_scale(q_cross, q_squares, gram_terms(q_down), q_up, q_magnitude)
    query_num = query_base + adapter_term(normed, q_down, q_up, onehot)
    row_scale = jnp.dot(onehot, q_scale, precision=PRECISE)
    query = rotate(query_num * row_scale, lengths).astype(jnp.bfloat16)
    w_keyval = dequantize(kv_codes, kv_absmax)
    keyval = jnp.dot(normed, w_keyval, preferred_element_type=jnp.float32)
    key_width = KV_HEADS * HEAD_DIM
    new_keys = rotate(keyval[:, :key_width], lengths).astype(jnp.bfloat16)
    new_values = keyval[:, key_width:].astype(jnp.bfloat16)
    group = HEADS // KV_HEADS
    inv_root = 1.0 / math.sqrt(HEAD_DIM)
    token_total = MAX_PAGES * PAGE

    def one_row(row_id):
        query_row = query[row_id].astype(jnp.float32).reshape(KV_HEADS, group, HEAD_DIM)
        pages = kv_cache[page_table[row_id]]
        key_rows = pages[:, 0].reshape(token_total, KV_HEADS, HEAD_DIM).astype(jnp.float32)
        value_rows = pages[:, 1].reshape(token_total, KV_HEADS, HEAD_DIM).astype(jnp.float32)
        scores = jnp.einsum('ghd,tgd->ght', query_row, key_rows, precision=PRECISE) * inv_root
        inside = jnp.arange(token_total, dtype=jnp.int32) < lengths[row_id]
        scores = jnp.where(inside[None, None, :], scores, NEG_FILL)
        own_key = new_keys[row_id].astype(jnp.float32).reshape(KV_HEADS, 1, HEAD_DIM)
        own_score = lax.optimization_barrier(jnp.sum(query_row * own_key, axis=-1)) * inv_root
        peak_score = jnp.maximum(lax.optimization_barrier(jnp.max(scores, axis=-1)), own_score)
        weights = jnp.where(inside[None, None, :], jnp.exp(scores - peak_score[..., None]), 0.0)
        own_weight = jnp.exp(own_score - peak_score)
        denominator = lax.optimization_barrier(jnp.sum(weights, axis=-1)) + own_weight
        own_value = new_values[row_id].astype(jnp.float32).reshape(KV_HEADS, 1, HEAD_DIM)
        numerator = jnp.einsum('ght,tgd->ghd', weights, value_rows, precision=PRECISE) + own_weight[..., None] * own_value
        return (numerator / denominator[..., None]).reshape(QWIDTH)
    attended = lax.map(one_row, jnp.arange(ROWS, dtype=jnp.int32)).astype(jnp.bfloat16)
    o_parts = column_pieces(o_codes, o_absmax, weight_terms(attended, o_down), N_GY)
    out_base, o_cross, o_squares = [join_columns(stacked_part) for stacked_part in o_parts]
    o_scale = column_scale(o_cross, o_squares, gram_terms(o_down), o_up, o_magnitude)
    out_num = out_base + adapter_term(attended, o_down, o_up, onehot)
    layer_out = states + out_num * jnp.dot(onehot, o_scale, precision=PRECISE)
    return layer_out.astype(jnp.bfloat16)
```

```python
import functools
import math

import jax
import jax.numpy as jnp
import numpy as np
from jax import lax
from jax.experimental import pallas as pl
from jax.experimental.pallas import tpu as pltpu
from jax.sharding import PartitionSpec as P

HEADS = 128
KV_HEADS = 8
HEAD_DIM = 128
TENANTS = 8
RANK = 16
QBLOCK = 64
PAGE = 256
ROWS = 8
NX = 8
NY = 16
SLOTS = 5
LOCAL_IN = 2048
HALF = 512
CHUNK = 256
CHUNKS = LOCAL_IN // CHUNK
D = 16384

NF4_LEVELS = (
    -1.0,
    -0.6961928009986877,
    -0.5250730514526367,
    -0.39491748809814453,
    -0.28444138169288635,
    -0.18477343022823334,
    -0.09105003625154495,
    0.0,
    0.07958029955625534,
    0.16093020141124725,
    0.24611230194568634,
    0.33791524171829224,
    0.44070982933044434,
    0.5626170039176941,
    0.7229568362236023,
    1.0,
)
NORM_EPS = 1e-05
NEG_FILL = -1e30
ROPE_BASE = 500000.0
MESH = pl.DeviceIdType.MESH
F32 = jnp.float32
BF16 = jnp.bfloat16
INV_ROOT = 1.0 / math.sqrt(HEAD_DIM)


def constants():
    table = np.zeros((16, 128), np.float32)
    table[:8, :16] = np.asarray(NF4_LEVELS, np.float32)[None]
    frequency = ROPE_BASE ** (-2.0 * np.arange(64, dtype=np.float64) / HEAD_DIM)
    table[8:] = np.concatenate([frequency, frequency]).astype(np.float32)[None]
    return table


def lookup(table, index):
    numbers = lax.GatherDimensionNumbers(
        offset_dims=(),
        collapsed_slice_dims=(1,),
        start_index_map=(1,),
        operand_batching_dims=(0,),
        start_indices_batching_dims=(0,),
    )
    return lax.gather(
        table,
        index[..., None],
        numbers,
        slice_sizes=(1, 1),
        mode=lax.GatherScatterMode.PROMISE_IN_BOUNDS,
    )


def lanes_of(shape):
    return lax.broadcasted_iota(jnp.int32, shape, 1)


def rows_of(shape):
    return lax.broadcasted_iota(jnp.int32, shape, 0)


def dot(a, b):
    return lax.dot_general(a, b, (((1,), (0,)), ((), ())), preferred_element_type=F32)


def dot_nt(a, b):
    return lax.dot_general(a, b, (((1,), (1,)), ((), ())), preferred_element_type=F32)


def two_parts(x):
    high = x.astype(BF16)
    return high, (x - high.astype(F32)).astype(BF16)


def parted(x):
    n, width = x.shape
    lane = lanes_of((n, 128))
    low = lane < 64
    evens, odds = [], []
    for c in range(width // 256):
        a, b = x[:, 256 * c : 256 * c + 128], x[:, 256 * c + 128 : 256 * c + 256]
        at = (2 * lane) & 127
        evens.append(jnp.where(low, lookup(a, at), lookup(b, at)))
        odds.append(jnp.where(low, lookup(a, at + 1), lookup(b, at + 1)))
    return jnp.concatenate(evens, axis=1), jnp.concatenate(odds, axis=1)


def joined(even, odd):
    n, width = even.shape
    lane = lanes_of((n, 128))
    is_even = (lane & 1) == 0
    blocks = []
    for c in range(width // 64):
        part = slice(128 * (c // 2), 128 * (c // 2) + 128)
        at = 64 * (c % 2) + (lane >> 1)
        blocks.append(jnp.where(is_even, lookup(even[:, part], at), lookup(odd[:, part], at)))
    return blocks


def kernel(
    tenant,
    lengths,
    hidden,
    gain,
    q_codes,
    q_absmax,
    kv_codes,
    kv_absmax,
    o_codes,
    o_absmax,
    q_down,
    q_up,
    q_magnitude,
    o_down,
    o_up,
    o_magnitude,
    pages,
    cache,
    consts,
    out,
    hid_v,
    gain_v,
    qc_v,
    qa_v,
    kc_v,
    ka_v,
    oc_v,
    oa_v,
    qd_v,
    qu_v,
    qm_v,
    od_v,
    ou_v,
    om_v,
    pt_v,
    cache_v,
    const_v,
    ae_v,
    ao_v,
    up_v,
    lhs_v,
    we_v,
    wo_v,
    acc_v,
    sq_v,
    flat_v,
    kvw_v,
    qf_v,
    score_v,
    num_v,
    nbf_v,
    att_v,
    b_src,
    b_dst,
    c1_src,
    c1_dst,
    c2_src,
    c2_dst,
    n_src,
    n_dst,
    s_src,
    s_dst,
    e2_src,
    e2_dst,
    e3_src,
    e3_dst,
    g_src,
    g_dst,
    load_sem,
    code_sem,
    page_sem,
    bs,
    br,
    c1s,
    c1r,
    c2s,
    c2r,
    ns,
    nr,
    ss,
    sr,
    e2s,
    e2r,
    e3s,
    e3r,
    gs,
    gr,
):
    gx = lax.axis_index("gx")
    gy = lax.axis_index("gy")

    def load(n, src, dst):
        copy = pltpu.make_async_copy(src, dst, load_sem.at[n])
        copy.start()
        return copy

    in_at = pl.multiple_of(gx * LOCAL_IN, LOCAL_IN)
    head_at = pl.multiple_of(gx * HEAD_DIM, HEAD_DIM)
    loads = [
        load(0, hidden, hid_v),
        load(1, gain.at[pl.ds(pl.multiple_of(gx * 16, 16), 16), :], gain_v),
        load(2, consts, const_v),
        load(3, q_absmax, qa_v),
        load(4, q_down, qd_v),
        load(5, q_up, qu_v),
    ]
    q_loads = []
    for c in range(CHUNKS):
        part = pl.ds(c * CHUNK, CHUNK)
        q_loads.append(pltpu.make_async_copy(q_codes.at[part, :], qc_v.at[part, :], code_sem.at[c]))
        q_loads[-1].start()
    later = [
        load(6, kv_codes, kc_v),
        load(7, kv_absmax, ka_v),
        load(8, q_magnitude.at[:, pl.ds(head_at, HEAD_DIM)], qm_v),
        load(9, pages, pt_v),
    ]
    o_small = [load(10, o_absmax, oa_v), load(11, o_down, od_v), load(12, o_up, ou_v), load(13, o_magnitude, om_v)]
    o_loads = []
    for c in range(CHUNKS):
        part = pl.ds(c * CHUNK, CHUNK)
        o_loads.append(
            pltpu.make_async_copy(o_codes.at[part, :], oc_v.at[part, :], code_sem.at[CHUNKS + c])
        )
        o_loads[-1].start()
    page_loads = []
    for s in range(SLOTS):
        page_loads.append(pltpu.make_async_copy(cache.at[s], cache_v.at[s], page_sem.at[s]))
        page_loads[-1].start()

    barrier = pltpu.get_barrier_semaphore()
    for k in range(1, NX):
        pl.semaphore_signal(
            barrier, inc=1, device_id={"gx": lax.rem(gx + k, NX)}, device_id_type=MESH
        )
    for k in range(1, NY):
        pl.semaphore_signal(
            barrier, inc=1, device_id={"gy": lax.rem(gy + k, NY)}, device_id_type=MESH
        )

    def to_gx(k, src, dst, send, recv):
        return pltpu.make_async_remote_copy(
            src_ref=src,
            dst_ref=dst,
            send_sem=send.at[k],
            recv_sem=recv.at[k],
            device_id={"gx": lax.rem(gx + k, NX)},
            device_id_type=MESH,
        )

    def to_gy(k, src, dst, send, recv):
        return pltpu.make_async_remote_copy(
            src_ref=src,
            dst_ref=dst,
            send_sem=send.at[k],
            recv_sem=recv.at[k],
            device_id={"gy": lax.rem(gy + k, NY)},
            device_id_type=MESH,
        )

    started = []

    for copy in loads:
        copy.wait()

    row8 = rows_of((ROWS, 128))
    lane8 = lanes_of((ROWS, 128))
    tenant_of = jnp.zeros((ROWS, 128), jnp.int32)
    length_of = jnp.zeros((ROWS, 128), jnp.int32)
    for r in range(ROWS):
        tenant_of = jnp.where(row8 == r, tenant[r], tenant_of)
        length_of = jnp.where(row8 == r, lengths[r], length_of)
    angles = length_of.astype(F32) * const_v[8:16, :]
    cosine = jnp.cos(angles)
    sine = jnp.sin(angles)
    sine = jnp.where(lane8 < 64, -sine, sine)

    def rope(x):
        return x * cosine + pltpu.roll(x, 64, 1) * sine

    total = jnp.zeros((ROWS, 128), F32)
    for c in range(D // 1024):
        x = hid_v[:, c * 1024 : (c + 1) * 1024].astype(F32)
        x = x * x
        for j in range(8):
            total = total + x[:, j * 128 : (j + 1) * 128]
    inverse = lax.rsqrt(jnp.sum(total, axis=1, keepdims=True) * (1.0 / D) + NORM_EPS)
    states = hid_v[:, pl.ds(in_at, LOCAL_IN)].astype(F32)
    lhs_v[0:16, :] = jnp.zeros((16, LOCAL_IN), BF16)
    normed = []
    for c in range(16):
        x = states[:, c * 128 : (c + 1) * 128] * inverse * gain_v[c : c + 1, :]
        normed.append(x)
    normed = jnp.concatenate(normed, axis=1)
    lhs_v[0:16, :] = jnp.concatenate([normed, jnp.zeros_like(normed)], axis=0).astype(BF16)
    lhs_v[16:144, :] = qd_v[...]

    lane64 = lanes_of((64, 128))
    table = jnp.broadcast_to(const_v[0:1, :], (64, 128))

    def dequantize(codes, row, scale_row):
        for c in range(4):
            cols = slice(128 * c, 128 * c + 128)
            words = codes[pl.ds(row, 64), cols]
            for half, (scales, ref) in enumerate(((ae_v, we_v), (ao_v, wo_v))):
                code = words & 15 if half == 0 else words >> 4
                value = lookup(table, code) * scales[c, pl.ds(scale_row, 1), :]
                ref[pl.ds(row, 64), cols] = value.astype(BF16)
                square = value * value
                part = square[0:8]
                for j in range(1, 8):
                    part = part + square[8 * j : 8 * j + 8]
                sq_v[half, :, cols] += part

    def weight_chunks(codes, first, last, lhs_rows):
        def chunk(c, carry):
            base = pl.multiple_of(c * CHUNK, CHUNK)
            for b in range(CHUNK // QBLOCK):
                row = pl.multiple_of(c * CHUNK + b * QBLOCK, QBLOCK)
                dequantize(codes, row, c * (CHUNK // QBLOCK) + b)
            left = lhs_v[lhs_rows, pl.ds(base, CHUNK)]
            acc_v[0, lhs_rows, :] += dot(left, we_v[pl.ds(base, CHUNK), :])
            acc_v[1, lhs_rows, :] += dot(left, wo_v[pl.ds(base, CHUNK), :])
            return carry

        lax.fori_loop(first, last, chunk, 0)

    def begin_projection(absmax, up):
        even, odd = parted(absmax[...])
        for c in range(4):
            ae_v[c] = even[:, 128 * c : 128 * c + 128]
            ao_v[c] = odd[:, 128 * c : 128 * c + 128]
        for c in range(4):
            even, odd = parted(up[:, 256 * c : 256 * c + 256].astype(F32))
            up_v[0, :, 128 * c : 128 * c + 128] = even.astype(BF16)
            up_v[1, :, 128 * c : 128 * c + 128] = odd.astype(BF16)
        acc_v[...] = jnp.zeros_like(acc_v)
        sq_v[...] = jnp.zeros_like(sq_v)

    def norm_parts(gram):
        same = (rows_of((128, 128)) >> 4) == (lanes_of((128, 128)) >> 4)
        high, low = two_parts(jnp.where(same, gram, 0.0))
        halves = []
        for half in range(2):
            up = up_v[half]
            inner = 2.0 * acc_v[half, 16:144, :] + (dot(high, up) + dot(low, up))
            terms = jnp.sum((up.astype(F32) * inner).reshape(TENANTS, RANK, HALF), axis=1)
            terms = terms + jnp.sum(sq_v[half], axis=0, keepdims=True)
            mine = tenant_of[:, 0:1]
            chosen = jnp.zeros((ROWS, HALF), F32)
            for t in range(TENANTS):
                chosen = jnp.where(mine == t, terms[t : t + 1, :], chosen)
            halves.append(chosen)
        return halves

    def adapter(middle):
        masked = jnp.where(tenant_of == (lane8 >> 4), middle, 0.0)
        high = masked.astype(BF16).astype(F32)
        both = jnp.concatenate([high, masked - high], axis=0).astype(BF16)
        halves = []
        for half in range(2):
            x = dot(both, up_v[half])
            halves.append(x[0:8] + x[8:16])
        return halves

    begin_projection(qa_v, qu_v)
    for copy in later:
        copy.wait()

    lane32 = lanes_of((32, 128))
    at = jnp.where(lane32 < 64, 2 * lane32, 2 * lane32 - 127)
    kv_scale = jnp.concatenate(
        [lookup(ka_v[...], at), jnp.zeros((96, 128), F32)], axis=0
    ).T
    for c in range(16):
        words = kc_v[:, c * 128 : (c + 1) * 128]
        for half in range(2):
            code = words & 15 if half == 0 else words >> 4
            scale = lookup(kv_scale[64 * half : 64 * half + 64], 2 * c + (lane64 >> 6))
            kvw_v[64 * half : 64 * half + 64, c * 128 : (c + 1) * 128] = (
                lookup(table, code) * scale
            ).astype(BF16)
    keyval = dot_nt(lhs_v[0:16, :], kvw_v[...])[0:8]
    keyval = lookup(keyval, jnp.where((lane8 & 1) == 0, lane8 >> 1, 64 + (lane8 >> 1)))

    inner = dot_nt(lhs_v[...], lhs_v[16:144, :])
    middle, gram = inner[0:8], inner[16:144]

    for copy in q_loads:
        copy.wait()
    weight_chunks(qc_v, 0, CHUNKS, slice(0, 144))

    extra = adapter(middle)
    product = joined(acc_v[0, 0:8, :] + extra[0], acc_v[1, 0:8, :] + extra[1])
    norms = joined(*norm_parts(gram))
    for i in range(NX):
        b_src[i, 0] = product[i]
        b_src[i, 1] = norms[i]
        b_src[i, 2] = keyval

    pl.semaphore_wait(barrier, NX - 1 + NY - 1)

    b_copies = []
    for k in range(1, NX):
        peer = lax.rem(gx + k, NX)
        b_copies.append(to_gx(k, b_src.at[peer], b_dst.at[k], bs, br))
        b_copies[-1].start()
    started += b_copies

    for copy in o_small:
        copy.wait()
    for copy in o_loads:
        copy.wait()
    begin_projection(oa_v, ou_v)
    lhs_v[16:144, :] = od_v[...]
    o_gram = dot_nt(lhs_v[16:144, :], lhs_v[16:144, :])
    down_rows = slice(16, 144)
    weight_chunks(oc_v, 0, 2, down_rows)

    summed = [b_src[gx, j] for j in range(3)]
    for copy in b_copies:
        copy.wait_recv()
    for k in range(1, NX):
        for j in range(3):
            summed[j] = summed[j] + b_dst[k, j]
    magnitude = jnp.zeros((ROWS, 128), F32)
    for t in range(TENANTS):
        magnitude = jnp.where(tenant_of == t, qm_v[t : t + 1, :], magnitude)
    query = rope(summed[0] * (magnitude * lax.rsqrt(summed[1])))
    new = jnp.where(gy < KV_HEADS, rope(summed[2]), summed[2])
    c1_src[...] = jnp.concatenate([query, new], axis=0).astype(BF16)
    c1_dst[gy] = c1_src[...]
    c1_copies = []
    for k in range(1, NY):
        c1_copies.append(to_gy(k, c1_src, c1_dst.at[gy], c1s, c1r))
        c1_copies[-1].start()
    started += c1_copies
    weight_chunks(oc_v, 2, 4, down_rows)

    for copy in c1_copies:
        copy.wait_recv()
    for j in range(NY // 2):
        pair = [c1_dst[2 * j + n].astype(F32)[0:8] for n in range(2)]
        c2_src[16 * j : 16 * j + 16, :] = jnp.concatenate(pair, axis=0).astype(BF16)
    c2_dst[gx] = c2_src[...]
    c2_copies = []
    for k in range(1, NX):
        c2_copies.append(to_gx(k, c2_src, c2_dst.at[gx], c2s, c2r))
        c2_copies[-1].start()
    started += c2_copies
    weight_chunks(oc_v, 4, CHUNKS, down_rows)
    o_norms = joined(*norm_parts(o_gram))
    for i in range(8):
        flat_v[8 * i : 8 * i + 8, :] = o_norms[i]
    for r in range(ROWS):
        g_src[r, 1] = flat_v[pl.ds(r, 8, stride=8), :]

    page_no = lanes_of((ROWS, 96))
    row_no = rows_of((ROWS, 96))
    length = length_of[:, 0:96]
    live = page_no * PAGE < length
    remaining = jnp.clip(length - page_no * PAGE, 0, PAGE)
    table_pages = pt_v[...]

    def whole(x):
        return jnp.sum(jnp.sum(x.astype(F32), axis=1, keepdims=True), axis=0, keepdims=True)

    owner, filled = [], []
    for s in range(SLOTS):
        hit = jnp.logical_and(table_pages == (gx * NY + gy) * SLOTS + s, live)
        owner.append(whole(jnp.where(hit, row_no, 0)))
        filled.append(whole(jnp.where(hit, remaining, 0)))

    def same(a, b):
        return jnp.where(a == b, 1.0, 0.0).astype(F32)

    for copy in c2_copies:
        copy.wait_recv()
    for i in range(NX):
        block = c2_dst[i].astype(F32)
        for j in range(NY):
            qf_v[pl.ds(8 * j + i, 8, stride=HEADS), :] = block[8 * j : 8 * j + 8]

    even_group = ((rows_of((HEADS, 128)) >> 4) & 1) == 0
    token = lanes_of((HEADS, PAGE)).astype(F32)
    peaks = []
    for s in range(SLOTS):
        q = jnp.zeros((HEADS, HEAD_DIM), F32)
        for r in range(ROWS):
            q = q + qf_v[r * HEADS : (r + 1) * HEADS, :] * same(owner[s], float(r))
        q = jnp.concatenate(
            [jnp.where(even_group, q, 0.0), jnp.where(even_group, 0.0, q)], axis=1
        ).astype(BF16)
        page_loads[s].wait()
        parts = [
            dot_nt(q[32 * p : 32 * p + 32], cache_v[s, 0, :, 256 * p : 256 * p + 256])
            for p in range(4)
        ]
        score = jnp.concatenate(parts, axis=0) * INV_ROOT
        score = jnp.where(token < filled[s], score, NEG_FILL)
        score_v[s] = score
        peaks.append(jnp.max(score, axis=1, keepdims=True))
    totals = []
    for s in range(SLOTS):
        peak = peaks[s]
        for other in range(SLOTS):
            if other != s:
                alike = owner[s] == owner[other]
                peak = jnp.maximum(peak, jnp.where(alike, peaks[other], NEG_FILL))
        weights = jnp.where(token < filled[s], jnp.exp(score_v[s] - peak), 0.0).astype(BF16)
        totals.append(jnp.sum(weights.astype(F32), axis=1, keepdims=True))
        for p in range(4):
            x = dot(weights[32 * p : 32 * p + 32], cache_v[s, 1, :, 256 * p : 256 * p + 256])
            num_v[s, 32 * p : 32 * p + 16, :] = x[0:16, 0:128]
            num_v[s, 32 * p + 16 : 32 * p + 32, :] = x[16:32, 128:256]
    lane_h = lanes_of((HEADS, 128))
    stats = jnp.zeros((HEADS, 128), F32)
    for r in range(ROWS):
        number = jnp.zeros((HEADS, HEAD_DIM), F32)
        peak = jnp.full((HEADS, 1), NEG_FILL, F32)
        total = jnp.zeros((HEADS, 1), F32)
        for s in range(SLOTS):
            mine = same(owner[s], float(r))
            number = number + num_v[s] * mine
            total = total + totals[s] * mine
            peak = jnp.maximum(peak, jnp.where(owner[s] == float(r), peaks[s], NEG_FILL))
        nbf_v[pl.ds(r, HEADS, stride=ROWS), :] = number
        stats = jnp.where(lane_h == r, peak, stats)
        stats = jnp.where(lane_h == 8 + r, total, stats)
    s_src[...] = stats.T[0:16]
    n_src[...] = nbf_v[...].astype(BF16)

    n_copies = []
    for k in range(1, NX):
        peer = lax.rem(gx + k, NX)
        part = pl.ds(pl.multiple_of(peer * 128, 128), 128)
        n_copies.append(to_gx(k, s_src, s_dst.at[k], ss, sr))
        n_copies[-1].start()
        n_copies.append(to_gx(k, n_src.at[part, :], n_dst.at[k], ns, nr))
        n_copies[-1].start()
    started += n_copies

    own_q = qf_v[pl.ds(16 * gx + gy, 8, stride=HEADS), :]
    new_key = c1_dst[gx].astype(F32)[8:16]
    new_value = c1_dst[KV_HEADS + gx].astype(F32)[8:16]
    self_score = jnp.sum(own_q * new_key, axis=1, keepdims=True) * INV_ROOT

    for copy in n_copies:
        copy.wait_recv()
    n_dst[0] = n_src[pl.ds(pl.multiple_of(gx * 128, 128), 128), :]
    s_dst[0] = s_src[...]
    peak = s_dst[0, 0:8]
    for k in range(1, NX):
        peak = jnp.maximum(peak, s_dst[k, 0:8])
    total = jnp.zeros((ROWS, 128), F32)
    shift = lax.rem(128 - 16 * gx, 128)
    factors = []
    for k in range(NX):
        factor = jnp.exp(s_dst[k, 0:8] - peak)
        total = total + factor * s_dst[k, 8:16]
        factors.append(pltpu.roll(factor, shift, 1))
    peak = pltpu.roll(peak, shift, 1)
    total = pltpu.roll(total, shift, 1)
    for j in range(NY // 2):
        pair = [jnp.zeros((ROWS, 128), F32), jnp.zeros((ROWS, 128), F32)]
        for k in range(NX):
            block = n_dst[k, 16 * j : 16 * j + 16, :].astype(F32)
            for n in range(2):
                h = 2 * j + n
                pair[n] = pair[n] + block[8 * n : 8 * n + 8] * factors[k][:, h : h + 1]
        for n in range(2):
            h = 2 * j + n
            e2_src[h, 0] = pair[n]
            e2_src[h, 1] = jnp.where(lane8 < 64, peak[:, h : h + 1], total[:, h : h + 1])

    e2_copies = []
    for k in range(1, NY):
        peer = lax.rem(gy + k, NY)
        e2_copies.append(to_gy(k, e2_src.at[peer], e2_dst.at[k], e2s, e2r))
        e2_copies[-1].start()
    started += e2_copies
    for copy in e2_copies:
        copy.wait_recv()
    e2_dst[0] = e2_src[gy]
    peak = self_score
    for k in range(NY):
        peak = jnp.maximum(peak, e2_dst[k, 1][:, 0:1])
    own = jnp.exp(self_score - peak)
    number = own * new_value
    total = own
    for k in range(NY):
        both = e2_dst[k, 1]
        factor = jnp.exp(both[:, 0:1] - peak)
        number = number + factor * e2_dst[k, 0]
        total = total + factor * both[:, 64:65]
    e3_src[...] = (number / total).astype(BF16).astype(F32)
    e3_dst[gy] = e3_src[...]
    e3_copies = []
    for k in range(1, NY):
        e3_copies.append(to_gy(k, e3_src, e3_dst.at[gy], e3s, e3r))
        e3_copies[-1].start()
    started += e3_copies
    for copy in e3_copies:
        copy.wait_recv()

    for j in range(NY):
        x = e3_dst[j]
        att_v[:, 128 * j : 128 * j + 128] = jnp.concatenate([x, jnp.zeros_like(x)], axis=0).astype(BF16)
    attended = att_v[...]
    middle = dot_nt(attended, lhs_v[16:144, :])[0:8]
    extra = adapter(middle)
    projected = joined(
        dot(attended, we_v[...])[0:8] + extra[0], dot(attended, wo_v[...])[0:8] + extra[1]
    )
    for i in range(8):
        flat_v[8 * i : 8 * i + 8, :] = projected[i]
    for r in range(ROWS):
        g_src[r, 0] = flat_v[pl.ds(r, 8, stride=8), :]
    g_copies = []
    for k in range(1, NX):
        peer = lax.rem(gx + k, NX)
        g_copies.append(to_gx(k, g_src.at[peer], g_dst.at[k], gs, gr))
        g_copies[-1].start()
    started += g_copies

    states = hid_v[:, pl.ds(pl.multiple_of(gy * 1024, 1024), 1024)].astype(F32)
    mine = tenant[gx]
    magnitude = jnp.zeros((8, 128), F32)
    for i in range(8):
        flat_v[8 * i : 8 * i + 8, :] = om_v[:, 128 * i : 128 * i + 128]
    for t in range(TENANTS):
        magnitude = jnp.where(mine == t, flat_v[pl.ds(t, 8, stride=8), :], magnitude)
    for i in range(8):
        flat_v[8 * i : 8 * i + 8, :] = states[:, 128 * i : 128 * i + 128]
    residual = flat_v[pl.ds(gx, 8, stride=8), :]
    summed = [g_src[gx, j] for j in range(2)]
    for copy in g_copies:
        copy.wait_recv()
    for k in range(1, NX):
        for j in range(2):
            summed[j] = summed[j] + g_dst[k, j]
    out[...] = residual + summed[0] * (magnitude * lax.rsqrt(summed[1]))
    for copy in started:
        copy.wait_send()


def local(
    hidden,
    norm_gain,
    q_codes,
    q_absmax,
    kv_codes,
    kv_absmax,
    o_codes,
    o_absmax,
    q_down,
    q_up,
    q_magnitude,
    o_down,
    o_up,
    o_magnitude,
    tenant,
    lengths,
    page_table,
    kv_cache,
):
    def down_rows(down):
        return jnp.transpose(down, (0, 2, 1)).reshape(TENANTS * RANK, LOCAL_IN)

    def up_rows(up):
        return up.reshape(TENANTS * RANK, 1024)

    vmem = pltpu.VMEM
    dma = pltpu.SemaphoreType.DMA
    hbm = pl.BlockSpec(memory_space=pl.ANY)
    smem = pl.BlockSpec(memory_space=pltpu.SMEM)
    scratch = [
        vmem((8, D), BF16),
        vmem((16, 128), F32),
        vmem((LOCAL_IN, HALF), jnp.int32),
        vmem((32, 1024), F32),
        vmem((64, LOCAL_IN), jnp.int32),
        vmem((32, 128), F32),
        vmem((LOCAL_IN, HALF), jnp.int32),
        vmem((32, 1024), F32),
        vmem((128, LOCAL_IN), BF16),
        vmem((128, 1024), BF16),
        vmem((8, 128), F32),
        vmem((128, LOCAL_IN), BF16),
        vmem((128, 1024), BF16),
        vmem((8, 1024), F32),
        vmem((8, 96), jnp.int32),
        vmem((SLOTS, 2, PAGE, 1024), BF16),
        vmem((16, 128), F32),
        vmem((4, 32, 128), F32),
        vmem((4, 32, 128), F32),
        vmem((2, 128, HALF), BF16),
        vmem((144, LOCAL_IN), BF16),
        vmem((LOCAL_IN, HALF), BF16),
        vmem((LOCAL_IN, HALF), BF16),
        vmem((2, 144, HALF), F32),
        vmem((2, 8, HALF), F32),
        vmem((64, 128), F32),
        vmem((128, LOCAL_IN), BF16),
        vmem((ROWS * HEADS, HEAD_DIM), F32),
        vmem((SLOTS, HEADS, PAGE), F32),
        vmem((SLOTS, HEADS, HEAD_DIM), F32),
        vmem((ROWS * HEADS, HEAD_DIM), F32),
        vmem((16, LOCAL_IN), BF16),
        vmem((NX, 3, 8, 128), F32),
        vmem((NX, 3, 8, 128), F32),
        vmem((16, 128), BF16),
        vmem((NY, 16, 128), BF16),
        vmem((128, 128), BF16),
        vmem((NX, 128, 128), BF16),
        vmem((ROWS * HEADS, HEAD_DIM), BF16),
        vmem((NX, 128, 128), BF16),
        vmem((16, 128), F32),
        vmem((NX, 16, 128), F32),
        vmem((NY, 2, 8, 128), F32),
        vmem((NY, 2, 8, 128), F32),
        vmem((8, 128), F32),
        vmem((NY, 8, 128), F32),
        vmem((NX, 2, 8, 128), F32),
        vmem((NX, 2, 8, 128), F32),
        dma((14,)),
        dma((2 * CHUNKS,)),
        dma((SLOTS,)),
        dma((NX,)),
        dma((NX,)),
        dma((NY,)),
        dma((NY,)),
        dma((NX,)),
        dma((NX,)),
        dma((NX,)),
        dma((NX,)),
        dma((NX,)),
        dma((NX,)),
        dma((NY,)),
        dma((NY,)),
        dma((NY,)),
        dma((NY,)),
        dma((NX,)),
        dma((NX,)),
    ]
    result = pl.pallas_call(
        kernel,
        out_shape=jax.ShapeDtypeStruct((8, 128), F32),
        in_specs=[smem, smem] + [hbm] * 17,
        out_specs=pl.BlockSpec(memory_space=pltpu.VMEM),
        scratch_shapes=scratch,
        compiler_params=pltpu.CompilerParams(
            collective_id=0, has_side_effects=True, vmem_limit_bytes=56 * 1024 * 1024
        ),
        name="layer",
    )(
        tenant,
        lengths,
        hidden,
        norm_gain.reshape(128, 128),
        q_codes,
        q_absmax,
        kv_codes.T,
        kv_absmax,
        o_codes,
        o_absmax,
        down_rows(q_down),
        up_rows(q_up),
        q_magnitude,
        down_rows(o_down),
        up_rows(o_up),
        o_magnitude,
        page_table,
        kv_cache,
        jnp.asarray(constants()),
    )
    return result.reshape(1, 1024).astype(BF16)


def solution(mesh):
    in_specs = (
        P(),
        P(),
        P("gx", "gy"),
        P("gx", "gy"),
        P("gx", "gy"),
        P("gx", "gy"),
        P("gx", "gy"),
        P("gx", "gy"),
        P(None, "gx", None),
        P(None, None, "gy"),
        P(None, "gy"),
        P(None, "gx", None),
        P(None, None, "gy"),
        P(None, "gy"),
        P(),
        P(),
        P(),
        P(("gx", "gy"), None, None, None),
    )
    return jax.shard_map(
        local, mesh=mesh, in_specs=in_specs, out_specs=P("gx", "gy"), check_vma=False
    )
```

```python
import functools
import math

import jax
import jax.numpy as jnp
import numpy as np
from jax import lax
from jax.experimental import pallas as pl
from jax.experimental.pallas import tpu as pltpu
from jax.sharding import PartitionSpec as P

HEADS = 128
KV_HEADS = 8
HEAD_DIM = 128
TENANTS = 8
RANK = 16
QBLOCK = 64
PAGE = 256
ROWS = 8
NX = 8
NY = 16
SLOTS = 5
LOCAL_IN = 2048
HALF = 512
CHUNK = 256
CHUNKS = LOCAL_IN // CHUNK
D = 16384

NF4_LEVELS = (
    -1.0,
    -0.6961928009986877,
    -0.5250730514526367,
    -0.39491748809814453,
    -0.28444138169288635,
    -0.18477343022823334,
    -0.09105003625154495,
    0.0,
    0.07958029955625534,
    0.16093020141124725,
    0.24611230194568634,
    0.33791524171829224,
    0.44070982933044434,
    0.5626170039176941,
    0.7229568362236023,
    1.0,
)
NORM_EPS = 1e-05
NEG_FILL = -1e30
ROPE_BASE = 500000.0
MESH = pl.DeviceIdType.MESH
F32 = jnp.float32
BF16 = jnp.bfloat16
INV_ROOT = 1.0 / math.sqrt(HEAD_DIM)


def constants():
    table = np.zeros((24, 128), np.float32)
    table[:16] = np.asarray(NF4_LEVELS, np.float32)[:, None]
    frequency = ROPE_BASE ** (-2.0 * np.arange(64, dtype=np.float64) / HEAD_DIM)
    table[16:] = np.concatenate([frequency, frequency]).astype(np.float32)[None]
    return table


def lookup(table, index):
    numbers = lax.GatherDimensionNumbers(
        offset_dims=(),
        collapsed_slice_dims=(1,),
        start_index_map=(1,),
        operand_batching_dims=(0,),
        start_indices_batching_dims=(0,),
    )
    return lax.gather(
        table,
        index[..., None],
        numbers,
        slice_sizes=(1, 1),
        mode=lax.GatherScatterMode.PROMISE_IN_BOUNDS,
    )


def levels(tables, code):
    numbers = lax.GatherDimensionNumbers(
        offset_dims=(),
        collapsed_slice_dims=(0,),
        start_index_map=(0,),
        operand_batching_dims=(1,),
        start_indices_batching_dims=(1,),
    )

    def pick(table, index):
        return lax.gather(
            table,
            index[..., None],
            numbers,
            slice_sizes=(1, 1),
            mode=lax.GatherScatterMode.PROMISE_IN_BOUNDS,
        )

    parts = []
    for j in range(code.shape[0] // 8):
        part = code[8 * j : 8 * j + 8]
        at = part & 7
        parts.append(jnp.where((part & 8) != 0, pick(tables[1], at), pick(tables[0], at)))
    return jnp.concatenate(parts, axis=0)


def lanes_of(shape):
    return lax.broadcasted_iota(jnp.int32, shape, 1)


def rows_of(shape):
    return lax.broadcasted_iota(jnp.int32, shape, 0)


def dot(a, b):
    return lax.dot_general(a, b, (((1,), (0,)), ((), ())), preferred_element_type=F32)


def dot_nt(a, b):
    return lax.dot_general(a, b, (((1,), (1,)), ((), ())), preferred_element_type=F32)


def two_parts(x):
    high = x.astype(BF16)
    return high, (x - high.astype(F32)).astype(BF16)


def three_parts(x):
    high = x.astype(BF16)
    rest = x - high.astype(F32)
    middle = rest.astype(BF16)
    return [high, middle, (rest - middle.astype(F32)).astype(BF16)]


def even_first():
    row, lane = rows_of((256, 256)), lanes_of((256, 256))
    return jnp.where(row == jnp.where(lane < 128, 2 * lane, 2 * lane - 255), 1.0, 0.0).astype(BF16)


def joined(even, odd):
    n, width = even.shape
    lane = lanes_of((n, 128))
    is_even = (lane & 1) == 0
    blocks = []
    for c in range(width // 64):
        part = slice(128 * (c // 2), 128 * (c // 2) + 128)
        at = 64 * (c % 2) + (lane >> 1)
        blocks.append(jnp.where(is_even, lookup(even[:, part], at), lookup(odd[:, part], at)))
    return blocks


def kernel(
    tenant,
    lengths,
    hidden,
    gain,
    q_codes,
    q_absmax,
    kv_codes,
    kv_absmax,
    o_codes,
    o_absmax,
    q_down,
    q_up,
    q_magnitude,
    o_down,
    o_up,
    o_magnitude,
    pages,
    cache,
    consts,
    out,
    hid_v,
    gain_v,
    qc_v,
    qa_v,
    kc_v,
    ka_v,
    oc_v,
    oa_v,
    qd_v,
    qu_v,
    qm_v,
    od_v,
    ou_v,
    om_v,
    pt_v,
    cache_v,
    const_v,
    ae_v,
    ao_v,
    up_v,
    lhs_v,
    we_v,
    wo_v,
    acc_v,
    sq_v,
    flat_v,
    kvw_v,
    qf_v,
    score_v,
    num_v,
    nbf_v,
    att_v,
    b_src,
    b_dst,
    z_src,
    z_dst,
    c1_src,
    c1_dst,
    c2_dst,
    n_src,
    n_dst,
    e_src,
    e_dst,
    g_src,
    g_dst,
    load_sem,
    code_sem,
    page_sem,
    bs,
    br,
    zs,
    zr,
    c1s,
    c1r,
    c2s,
    c2r,
    ns,
    nr,
    es,
    er,
    gs,
    gr,
):
    gx = lax.axis_index("gx")
    gy = lax.axis_index("gy")

    def load(n, src, dst):
        copy = pltpu.make_async_copy(src, dst, load_sem.at[n])
        copy.start()
        return copy

    in_at = pl.multiple_of(gx * LOCAL_IN, LOCAL_IN)
    core = lax.rem(gx, 2)
    partner = gx + 1 - 2 * core
    z = lax.div(gx, 2)
    heads_at = pl.multiple_of(core * HALF, HALF)
    loads = [
        load(0, hidden, hid_v),
        load(1, gain.at[pl.ds(pl.multiple_of(gx * 16, 16), 16), :], gain_v),
        load(2, consts, const_v),
        load(4, q_down, qd_v),
        load(6, kv_codes, kc_v),
        load(7, kv_absmax, ka_v),
        load(3, q_absmax, qa_v),
        load(5, q_up, qu_v),
    ]
    q_loads = []
    for c in range(CHUNKS):
        part = pl.ds(c * CHUNK, CHUNK)
        q_loads.append(pltpu.make_async_copy(q_codes.at[part, :], qc_v.at[part, :], code_sem.at[c]))
        q_loads[-1].start()
    later = [
        load(8, q_magnitude.at[:, pl.ds(heads_at, HALF)], qm_v),
        load(9, pages, pt_v),
    ]
    o_small = [load(10, o_absmax, oa_v), load(11, o_down, od_v), load(12, o_up, ou_v), load(13, o_magnitude, om_v)]
    o_loads = []
    for c in range(CHUNKS):
        part = pl.ds(c * CHUNK, CHUNK)
        o_loads.append(
            pltpu.make_async_copy(o_codes.at[part, :], oc_v.at[part, :], code_sem.at[CHUNKS + c])
        )
        o_loads[-1].start()
    page_loads = []
    for s in range(SLOTS):
        page_loads.append(pltpu.make_async_copy(cache.at[s], cache_v.at[s], page_sem.at[s]))
        page_loads[-1].start()

    barrier = pltpu.get_barrier_semaphore()
    for k in range(1, NX):
        pl.semaphore_signal(
            barrier, inc=1, device_id={"gx": lax.rem(gx + k, NX)}, device_id_type=MESH
        )
    for k in range(1, NY):
        pl.semaphore_signal(
            barrier, inc=1, device_id={"gy": lax.rem(gy + k, NY)}, device_id_type=MESH
        )

    def to_partner(src, dst, send, recv):
        return pltpu.make_async_remote_copy(
            src_ref=src,
            dst_ref=dst,
            send_sem=send.at[0],
            recv_sem=recv.at[0],
            device_id={"gx": partner},
            device_id_type=MESH,
        )

    def to_gx(k, src, dst, send, recv):
        return pltpu.make_async_remote_copy(
            src_ref=src,
            dst_ref=dst,
            send_sem=send.at[k],
            recv_sem=recv.at[k],
            device_id={"gx": lax.rem(gx + k, NX)},
            device_id_type=MESH,
        )

    def to_gy(k, src, dst, send, recv):
        return pltpu.make_async_remote_copy(
            src_ref=src,
            dst_ref=dst,
            send_sem=send.at[k],
            recv_sem=recv.at[k],
            device_id={"gy": lax.rem(gy + k, NY)},
            device_id_type=MESH,
        )

    started = []

    row8 = rows_of((ROWS, 128))
    lane8 = lanes_of((ROWS, 128))
    tenant_of = jnp.zeros((ROWS, 128), jnp.int32)
    length_of = jnp.zeros((ROWS, 128), jnp.int32)
    for r in range(ROWS):
        tenant_of = jnp.where(row8 == r, tenant[r], tenant_of)
        length_of = jnp.where(row8 == r, lengths[r], length_of)
    for copy in loads[0:3]:
        copy.wait()
    angles = length_of.astype(F32) * const_v[16:24, :]
    cosine = jnp.cos(angles)
    sine = jnp.sin(angles)
    sine = jnp.where(lane8 < 64, -sine, sine)

    def rope(x):
        return x * cosine + pltpu.roll(x, 64, 1) * sine

    total = jnp.zeros((ROWS, 128), F32)
    for c in range(D // 1024):
        x = hid_v[:, c * 1024 : (c + 1) * 1024].astype(F32)
        x = x * x
        for j in range(8):
            total = total + x[:, j * 128 : (j + 1) * 128]
    inverse = lax.rsqrt(jnp.sum(total, axis=1, keepdims=True) * (1.0 / D) + NORM_EPS)
    states = hid_v[:, pl.ds(in_at, LOCAL_IN)].astype(F32)
    lhs_v[0:16, :] = jnp.zeros((16, LOCAL_IN), BF16)
    normed = []
    for c in range(16):
        x = states[:, c * 128 : (c + 1) * 128] * inverse * gain_v[c : c + 1, :]
        normed.append(x)
    normed = jnp.concatenate(normed, axis=1)
    lhs_v[0:16, :] = jnp.concatenate([normed, jnp.zeros_like(normed)], axis=0).astype(BF16)
    for copy in loads[3:]:
        copy.wait()
    lhs_v[16:144, :] = qd_v[...]

    lane64 = lanes_of((64, 128))
    tables = (const_v[0:8, :], const_v[8:16, :])
    parting = even_first()

    def dequantize(codes, row, scale_row):
        for c in range(4):
            cols = slice(128 * c, 128 * c + 128)
            words = codes[pl.ds(row, 64), cols]
            for half, (scales, ref) in enumerate(((ae_v, we_v), (ao_v, wo_v))):
                code = words & 15 if half == 0 else words >> 4
                value = levels(tables, code) * scales[c, pl.ds(scale_row, 1), :]
                ref[pl.ds(row, 64), cols] = value.astype(BF16)
                square = value * value
                part = square[0:8]
                for j in range(1, 8):
                    part = part + square[8 * j : 8 * j + 8]
                sq_v[half, :, cols] += part

    def weight_chunk(codes, c, lhs_rows):
        base = c * CHUNK if isinstance(c, int) else pl.multiple_of(c * CHUNK, CHUNK)
        for b in range(CHUNK // QBLOCK):
            row = c * CHUNK + b * QBLOCK
            row = row if isinstance(c, int) else pl.multiple_of(row, QBLOCK)
            dequantize(codes, row, c * (CHUNK // QBLOCK) + b)
        left = lhs_v[lhs_rows, pl.ds(base, CHUNK)]
        acc_v[0, lhs_rows, :] += dot(left, we_v[pl.ds(base, CHUNK), :])
        acc_v[1, lhs_rows, :] += dot(left, wo_v[pl.ds(base, CHUNK), :])

    def weight_chunks(codes, first, last, lhs_rows):
        def step(c, carry):
            weight_chunk(codes, c, lhs_rows)
            return carry

        lax.fori_loop(first, last, step, 0)

    def begin_projection(absmax, up):
        for c in range(4):
            part = slice(256 * c, 256 * c + 256)
            parts = dot(jnp.concatenate(three_parts(absmax[:, part]), axis=0), parting)
            whole = parts[0:32] + parts[32:64] + parts[64:96]
            ae_v[c] = whole[:, 0:128]
            ao_v[c] = whole[:, 128:256]
            both = dot(up[:, part], parting).astype(BF16)
            up_v[0, :, 128 * c : 128 * c + 128] = both[:, 0:128]
            up_v[1, :, 128 * c : 128 * c + 128] = both[:, 128:256]
        acc_v[...] = jnp.zeros_like(acc_v)
        sq_v[...] = jnp.zeros_like(sq_v)

    def norm_parts(gram):
        same = (rows_of((128, 128)) >> 4) == (lanes_of((128, 128)) >> 4)
        high, low = two_parts(jnp.where(same, gram, 0.0))
        halves = []
        for half in range(2):
            up = up_v[half]
            inner = 2.0 * acc_v[half, 16:144, :] + (dot(high, up) + dot(low, up))
            terms = jnp.sum((up.astype(F32) * inner).reshape(TENANTS, RANK, HALF), axis=1)
            terms = terms + jnp.sum(sq_v[half], axis=0, keepdims=True)
            mine = tenant_of[:, 0:1]
            chosen = jnp.zeros((ROWS, HALF), F32)
            for t in range(TENANTS):
                chosen = jnp.where(mine == t, terms[t : t + 1, :], chosen)
            halves.append(chosen)
        return halves

    def adapter(middle):
        masked = jnp.where(tenant_of == (lane8 >> 4), middle, 0.0)
        high = masked.astype(BF16).astype(F32)
        both = jnp.concatenate([high, masked - high], axis=0).astype(BF16)
        halves = []
        for half in range(2):
            x = dot(both, up_v[half])
            halves.append(x[0:8] + x[8:16])
        return halves

    begin_projection(qa_v, qu_v)

    lane32 = lanes_of((32, 128))
    at = jnp.where(lane32 < 64, 2 * lane32, 2 * lane32 - 127)
    kv_scale = jnp.concatenate(
        [lookup(ka_v[...], at), jnp.zeros((96, 128), F32)], axis=0
    ).T
    for c in range(16):
        words = kc_v[:, c * 128 : (c + 1) * 128]
        for half in range(2):
            code = words & 15 if half == 0 else words >> 4
            scale = lookup(kv_scale[64 * half : 64 * half + 64], 2 * c + (lane64 >> 6))
            kvw_v[64 * half : 64 * half + 64, c * 128 : (c + 1) * 128] = (
                levels(tables, code) * scale
            ).astype(BF16)
    keyval = dot_nt(lhs_v[0:16, :], kvw_v[...])[0:8]
    keyval = lookup(keyval, jnp.where((lane8 & 1) == 0, lane8 >> 1, 64 + (lane8 >> 1)))

    inner = dot_nt(lhs_v[...], lhs_v[16:144, :])
    middle, gram = inner[0:8], inner[16:144]

    for c in range(CHUNKS):
        q_loads[c].wait()
        weight_chunk(qc_v, c, slice(0, 144))

    extra = adapter(middle)
    product = joined(acc_v[0, 0:8, :] + extra[0], acc_v[1, 0:8, :] + extra[1])
    norms = joined(*norm_parts(gram))
    for half in range(2):
        for m in range(4):
            b_src[half, m] = product[4 * half + m]
            b_src[half, 4 + m] = norms[4 * half + m]
        b_src[half, 8] = keyval

    pl.semaphore_wait(barrier, NX - 1 + NY - 1)

    b_copy = to_partner(b_src.at[1 - core], b_dst, bs, br)
    b_copy.start()
    started.append(b_copy)
    for copy in o_small:
        copy.wait()
    lhs_v[16:144, :] = od_v[...]
    o_gram = dot_nt(lhs_v[16:144, :], lhs_v[16:144, :])
    b_copy.wait_recv()
    z_src[...] = b_src[core] + b_dst[...]
    z_dst[z] = z_src[...]
    z_copies = []
    for k in range(1, 4):
        z_copies.append(to_gx(2 * k, z_src, z_dst.at[z], zs, zr))
        z_copies[-1].start()
    started += z_copies

    begin_projection(oa_v, ou_v)
    for copy in o_loads:
        copy.wait()
    down_rows = slice(16, 144)
    weight_chunks(oc_v, 0, 3, down_rows)

    for copy in later:
        copy.wait()
    for copy in z_copies:
        copy.wait_recv()
    summed = z_dst[0]
    for k in range(1, 4):
        summed = summed + z_dst[k]
    queries = []
    for m in range(4):
        magnitude = jnp.zeros((ROWS, 128), F32)
        for t in range(TENANTS):
            magnitude = jnp.where(
                tenant_of == t, qm_v[t : t + 1, 128 * m : 128 * m + 128], magnitude
            )
        queries.append(rope(summed[m] * (magnitude * lax.rsqrt(summed[4 + m]))))
    new = jnp.where(gy < KV_HEADS, rope(summed[8]), summed[8])
    c1_src[0:16, :] = jnp.concatenate(queries[0:2], axis=0).astype(BF16)
    c1_src[16:32, :] = jnp.concatenate(queries[2:4], axis=0).astype(BF16)
    c1_src[32:48, :] = jnp.concatenate([new, jnp.zeros_like(new)], axis=0).astype(BF16)
    c1_dst[gy] = c1_src[...]
    c1_copies = []
    for k in range(1, NY):
        c1_copies.append(to_gy(k, c1_src, c1_dst.at[gy], c1s, c1r))
        c1_copies[-1].start()
    started += c1_copies
    weight_chunks(oc_v, 3, CHUNKS, down_rows)
    o_norms = joined(*norm_parts(o_gram))
    for i in range(8):
        flat_v[8 * i : 8 * i + 8, :] = o_norms[i]
    for r in range(ROWS):
        g_src[r, 1] = flat_v[pl.ds(r, 8, stride=8), :]

    page_no = lanes_of((ROWS, 96))
    row_no = rows_of((ROWS, 96))
    length = length_of[:, 0:96]
    live = page_no * PAGE < length
    remaining = jnp.clip(length - page_no * PAGE, 0, PAGE)
    table_pages = pt_v[...]

    def whole(x):
        return jnp.sum(jnp.sum(x.astype(F32), axis=1, keepdims=True), axis=0, keepdims=True)

    owner, filled = [], []
    for s in range(SLOTS):
        hit = jnp.logical_and(table_pages == (gx * NY + gy) * SLOTS + s, live)
        owner.append(whole(jnp.where(hit, row_no, 0)))
        filled.append(whole(jnp.where(hit, remaining, 0)))

    def same(a, b):
        return jnp.where(a == b, 1.0, 0.0).astype(F32)

    for copy in c1_copies:
        copy.wait_recv()
    c2_copy = to_partner(c1_dst.at[:, 0:32, :], c2_dst, c2s, c2r)
    c2_copy.start()
    started.append(c2_copy)
    for j in range(NY):
        block = c1_dst[j].astype(F32)
        for m in range(4):
            qf_v[pl.ds(8 * j + 4 * core + m, 8, stride=HEADS), :] = block[8 * m : 8 * m + 8]
    c2_copy.wait_recv()
    for j in range(NY):
        block = c2_dst[j].astype(F32)
        for m in range(4):
            qf_v[pl.ds(8 * j + 4 - 4 * core + m, 8, stride=HEADS), :] = block[8 * m : 8 * m + 8]

    even_group = ((rows_of((HEADS, 128)) >> 4) & 1) == 0
    token = lanes_of((HEADS, PAGE)).astype(F32)
    peaks = []
    for s in range(SLOTS):
        q = jnp.zeros((HEADS, HEAD_DIM), F32)
        for r in range(ROWS):
            q = q + qf_v[r * HEADS : (r + 1) * HEADS, :] * same(owner[s], float(r))
        q = jnp.concatenate(
            [jnp.where(even_group, q, 0.0), jnp.where(even_group, 0.0, q)], axis=1
        ).astype(BF16)
        page_loads[s].wait()
        parts = [
            dot_nt(q[32 * p : 32 * p + 32], cache_v[s, 0, :, 256 * p : 256 * p + 256])
            for p in range(4)
        ]
        score = jnp.concatenate(parts, axis=0) * INV_ROOT
        score = jnp.where(token < filled[s], score, NEG_FILL)
        score_v[s] = score
        peaks.append(jnp.max(score, axis=1, keepdims=True))
    totals = []
    for s in range(SLOTS):
        peak = peaks[s]
        for other in range(SLOTS):
            if other != s:
                alike = owner[s] == owner[other]
                peak = jnp.maximum(peak, jnp.where(alike, peaks[other], NEG_FILL))
        weights = jnp.where(token < filled[s], jnp.exp(score_v[s] - peak), 0.0).astype(BF16)
        totals.append(jnp.sum(weights.astype(F32), axis=1, keepdims=True))
        for p in range(4):
            x = dot(weights[32 * p : 32 * p + 32], cache_v[s, 1, :, 256 * p : 256 * p + 256])
            num_v[s, 32 * p : 32 * p + 16, :] = x[0:16, 0:128]
            num_v[s, 32 * p + 16 : 32 * p + 32, :] = x[16:32, 128:256]
    lane_h = lanes_of((HEADS, 128))
    stats = jnp.zeros((HEADS, 128), F32)
    for r in range(ROWS):
        number = jnp.zeros((HEADS, HEAD_DIM), F32)
        peak = jnp.full((HEADS, 1), NEG_FILL, F32)
        total = jnp.zeros((HEADS, 1), F32)
        for s in range(SLOTS):
            mine = same(owner[s], float(r))
            number = number + num_v[s] * mine
            total = total + totals[s] * mine
            peak = jnp.maximum(peak, jnp.where(owner[s] == float(r), peaks[s], NEG_FILL))
        nbf_v[pl.ds(r, HEADS, stride=ROWS), :] = number
        stats = jnp.where(lane_h == r, peak, stats)
        stats = jnp.where(lane_h == 8 + r, total, stats)
    stats = three_parts(stats.T[0:16])
    stats = [x.astype(F32) for x in stats]
    lane16 = lanes_of((16, 128))
    for i in range(NX):
        n_src[i, 0:128, :] = nbf_v[128 * i : 128 * i + 128, :].astype(BF16)
        mine = [pltpu.roll(x, (16 * n - 16 * i) % 128, 1) if (n - i) % 8 else x for n, x in enumerate(stats)]
        n_src[i, 128:144, :] = jnp.where(
            lane16 < 16, mine[0], jnp.where(lane16 < 32, mine[1], mine[2])
        ).astype(BF16)

    n_copies = []
    for k in range(1, NX):
        peer = lax.rem(gx + k, NX)
        n_copies.append(to_gx(k, n_src.at[peer], n_dst.at[k], ns, nr))
        n_copies[-1].start()
    started += n_copies

    new_key = c1_dst[gx].astype(F32)[32:40]
    new_value = c1_dst[KV_HEADS + gx].astype(F32)[32:40]
    self_score = jnp.zeros((ROWS, 128), F32)
    for h in range(16):
        q = qf_v[pl.ds(16 * gx + h, 8, stride=HEADS), :]
        score = jnp.sum(q * new_key, axis=1, keepdims=True) * INV_ROOT
        self_score = jnp.where(lane8 == h, score, self_score)

    states = hid_v[:, pl.ds(pl.multiple_of(gy * 1024, 1024), 1024)].astype(F32)
    mine = tenant[gx]
    out_magnitude = jnp.zeros((8, 128), F32)
    for i in range(8):
        flat_v[8 * i : 8 * i + 8, :] = om_v[:, 128 * i : 128 * i + 128]
    for t in range(TENANTS):
        out_magnitude = jnp.where(mine == t, flat_v[pl.ds(t, 8, stride=8), :], out_magnitude)
    for i in range(8):
        flat_v[8 * i : 8 * i + 8, :] = states[:, 128 * i : 128 * i + 128]
    residual = flat_v[pl.ds(gx, 8, stride=8), :]

    def gathered(x, first):
        parts = [pltpu.roll(x, 128 - first - 16 * n, 1) if first + n else x for n in range(3)]
        return parts[0] + parts[1] + parts[2]

    for copy in n_copies:
        copy.wait_recv()
    n_dst[0] = n_src[gx]
    seen = [gathered(n_dst[k, 128:144, :].astype(F32), 0) for k in range(NX)]
    peak = seen[0][0:8]
    for k in range(1, NX):
        peak = jnp.maximum(peak, seen[k][0:8])
    total = jnp.zeros((ROWS, 128), F32)
    factors = []
    for k in range(NX):
        factors.append(jnp.exp(seen[k][0:8] - peak))
        total = total + factors[k] * seen[k][8:16]
    for j in range(8):
        pair = [jnp.zeros((ROWS, 128), F32), jnp.zeros((ROWS, 128), F32)]
        for k in range(NX):
            block = n_dst[k, 16 * j : 16 * j + 16, :].astype(F32)
            for n in range(2):
                h = 2 * j + n
                pair[n] = pair[n] + block[8 * n : 8 * n + 8] * factors[k][:, h : h + 1]
        e_src[16 * j : 16 * j + 16, :] = jnp.concatenate(pair, axis=0).astype(BF16)
    stats = jnp.zeros((ROWS, 128), F32)
    for n, x in enumerate(three_parts(peak) + three_parts(total)):
        x = x.astype(F32)
        x = pltpu.roll(x, 16 * n, 1) if n else x
        stats = jnp.where(jnp.logical_and(lane8 >= 16 * n, lane8 < 16 * n + 16), x, stats)
    e_src[128:144, :] = jnp.concatenate([stats, jnp.zeros_like(stats)], axis=0).astype(BF16)

    e_dst[gy] = e_src[...]
    e_copies = []
    for k in range(1, NY):
        e_copies.append(to_gy(k, e_src, e_dst.at[gy], es, er))
        e_copies[-1].start()
    started += e_copies
    for copy in e_copies:
        copy.wait_recv()
    peaks, totals = [], []
    peak = self_score
    for k in range(NY):
        x = e_dst[k, 128:144, :].astype(F32)[0:8]
        peaks.append(gathered(x, 0))
        totals.append(gathered(x, 48))
        peak = jnp.maximum(peak, peaks[k])
    own = jnp.exp(self_score - peak)
    total = own
    factors = []
    for k in range(NY):
        factors.append(jnp.exp(peaks[k] - peak))
        total = total + factors[k] * totals[k]
    for j in range(8):
        pair = [own[:, 2 * j + n : 2 * j + n + 1] * new_value for n in range(2)]
        for k in range(NY):
            block = e_dst[k, 16 * j : 16 * j + 16, :].astype(F32)
            for n in range(2):
                h = 2 * j + n
                pair[n] = pair[n] + block[8 * n : 8 * n + 8] * factors[k][:, h : h + 1]
        for n in range(2):
            h = 2 * j + n
            x = pair[n] / total[:, h : h + 1]
            att_v[:, 128 * h : 128 * h + 128] = jnp.concatenate([x, jnp.zeros_like(x)], axis=0).astype(BF16)

    attended = att_v[...]
    middle = dot_nt(attended, lhs_v[16:144, :])[0:8]
    extra = adapter(middle)
    projected = joined(
        dot(attended, we_v[...])[0:8] + extra[0], dot(attended, wo_v[...])[0:8] + extra[1]
    )
    for i in range(8):
        flat_v[8 * i : 8 * i + 8, :] = projected[i]
    for r in range(ROWS):
        g_src[r, 0] = flat_v[pl.ds(r, 8, stride=8), :]
    g_copies = []
    for k in range(1, NX):
        peer = lax.rem(gx + k, NX)
        g_copies.append(to_gx(k, g_src.at[peer], g_dst.at[k], gs, gr))
        g_copies[-1].start()
    started += g_copies

    summed = [g_src[gx, j] for j in range(2)]
    for copy in g_copies:
        copy.wait_recv()
    for k in range(1, NX):
        for j in range(2):
            summed[j] = summed[j] + g_dst[k, j]
    result = (residual + summed[0] * (out_magnitude * lax.rsqrt(summed[1]))).astype(BF16)
    out[...] = result
    for copy in started:
        copy.wait_send()


def local(
    hidden,
    norm_gain,
    q_codes,
    q_absmax,
    kv_codes,
    kv_absmax,
    o_codes,
    o_absmax,
    q_down,
    q_up,
    q_magnitude,
    o_down,
    o_up,
    o_magnitude,
    tenant,
    lengths,
    page_table,
    kv_cache,
):
    def down_rows(down):
        return jnp.transpose(down, (0, 2, 1)).reshape(TENANTS * RANK, LOCAL_IN)

    def up_rows(up):
        return up.reshape(TENANTS * RANK, 1024)

    vmem = pltpu.VMEM
    dma = pltpu.SemaphoreType.DMA
    hbm = pl.BlockSpec(memory_space=pl.ANY)
    smem = pl.BlockSpec(memory_space=pltpu.SMEM)
    scratch = [
        vmem((8, D), BF16),
        vmem((16, 128), F32),
        vmem((LOCAL_IN, HALF), jnp.int32),
        vmem((32, 1024), F32),
        vmem((64, LOCAL_IN), jnp.int32),
        vmem((32, 128), F32),
        vmem((LOCAL_IN, HALF), jnp.int32),
        vmem((32, 1024), F32),
        vmem((128, LOCAL_IN), BF16),
        vmem((128, 1024), BF16),
        vmem((8, HALF), F32),
        vmem((128, LOCAL_IN), BF16),
        vmem((128, 1024), BF16),
        vmem((8, 1024), F32),
        vmem((8, 96), jnp.int32),
        vmem((SLOTS, 2, PAGE, 1024), BF16),
        vmem((24, 128), F32),
        vmem((4, 32, 128), F32),
        vmem((4, 32, 128), F32),
        vmem((2, 128, HALF), BF16),
        vmem((144, LOCAL_IN), BF16),
        vmem((LOCAL_IN, HALF), BF16),
        vmem((LOCAL_IN, HALF), BF16),
        vmem((2, 144, HALF), F32),
        vmem((2, 8, HALF), F32),
        vmem((64, 128), F32),
        vmem((128, LOCAL_IN), BF16),
        vmem((ROWS * HEADS, HEAD_DIM), F32),
        vmem((SLOTS, HEADS, PAGE), F32),
        vmem((SLOTS, HEADS, HEAD_DIM), F32),
        vmem((ROWS * HEADS, HEAD_DIM), F32),
        vmem((16, LOCAL_IN), BF16),
        vmem((2, 9, 8, 128), F32),
        vmem((9, 8, 128), F32),
        vmem((9, 8, 128), F32),
        vmem((4, 9, 8, 128), F32),
        vmem((48, 128), BF16),
        vmem((NY, 48, 128), BF16),
        vmem((NY, 32, 128), BF16),
        vmem((NX, 144, 128), BF16),
        vmem((NX, 144, 128), BF16),
        vmem((144, 128), BF16),
        vmem((NY, 144, 128), BF16),
        vmem((NX, 2, 8, 128), F32),
        vmem((NX, 2, 8, 128), F32),
        dma((14,)),
        dma((2 * CHUNKS,)),
        dma((SLOTS,)),
        dma((1,)),
        dma((1,)),
        dma((NX,)),
        dma((NX,)),
        dma((NY,)),
        dma((NY,)),
        dma((1,)),
        dma((1,)),
        dma((NX,)),
        dma((NX,)),
        dma((NY,)),
        dma((NY,)),
        dma((NX,)),
        dma((NX,)),
    ]
    result = pl.pallas_call(
        kernel,
        out_shape=jax.ShapeDtypeStruct((8, 128), BF16),
        in_specs=[smem, smem] + [hbm] * 17,
        out_specs=pl.BlockSpec(memory_space=pltpu.VMEM),
        scratch_shapes=scratch,
        compiler_params=pltpu.CompilerParams(
            collective_id=0, has_side_effects=True, vmem_limit_bytes=56 * 1024 * 1024
        ),
        name="layer",
    )(
        tenant,
        lengths,
        hidden,
        norm_gain.reshape(128, 128),
        q_codes,
        q_absmax,
        kv_codes.T,
        kv_absmax,
        o_codes,
        o_absmax,
        down_rows(q_down),
        up_rows(q_up),
        q_magnitude,
        down_rows(o_down),
        up_rows(o_up),
        o_magnitude,
        page_table,
        kv_cache,
        jnp.asarray(constants()),
    )
    return result.reshape(1, 1024)


def solution(mesh):
    in_specs = (
        P(),
        P(),
        P("gx", "gy"),
        P("gx", "gy"),
        P("gx", "gy"),
        P("gx", "gy"),
        P("gx", "gy"),
        P("gx", "gy"),
        P(None, "gx", None),
        P(None, None, "gy"),
        P(None, "gy"),
        P(None, "gx", None),
        P(None, None, "gy"),
        P(None, "gy"),
        P(),
        P(),
        P(),
        P(("gx", "gy"), None, None, None),
    )
    return jax.shard_map(
        local, mesh=mesh, in_specs=in_specs, out_specs=P("gx", "gy"), check_vma=False
    )
```

```python
import functools
import math

import jax
import jax.numpy as jnp
import numpy as np
from jax import lax
from jax.experimental import pallas as pl
from jax.experimental.pallas import tpu as pltpu
from jax.sharding import PartitionSpec as P

HEADS = 128
KV_HEADS = 8
HEAD_DIM = 128
TENANTS = 8
RANK = 16
QBLOCK = 64
PAGE = 256
ROWS = 8
NX = 8
NY = 16
SLOTS = 5
LOCAL_IN = 2048
HALF = 512
CHUNK = 256
CHUNKS = LOCAL_IN // CHUNK
LATER = 5
FIRST = 2
D = 16384

NF4_LEVELS = (
    -1.0,
    -0.6961928009986877,
    -0.5250730514526367,
    -0.39491748809814453,
    -0.28444138169288635,
    -0.18477343022823334,
    -0.09105003625154495,
    0.0,
    0.07958029955625534,
    0.16093020141124725,
    0.24611230194568634,
    0.33791524171829224,
    0.44070982933044434,
    0.5626170039176941,
    0.7229568362236023,
    1.0,
)
NORM_EPS = 1e-05
NEG_FILL = -1e30
ROPE_BASE = 500000.0
MESH = pl.DeviceIdType.MESH
F32 = jnp.float32
BF16 = jnp.bfloat16
INV_ROOT = 1.0 / math.sqrt(HEAD_DIM)


def constants():
    table = np.zeros((24, 128), np.float32)
    table[:16] = np.asarray(NF4_LEVELS, np.float32)[:, None]
    frequency = ROPE_BASE ** (-2.0 * np.arange(64, dtype=np.float64) / HEAD_DIM)
    table[16:] = np.concatenate([frequency, frequency]).astype(np.float32)[None]
    return table


def lookup(table, index):
    numbers = lax.GatherDimensionNumbers(
        offset_dims=(),
        collapsed_slice_dims=(1,),
        start_index_map=(1,),
        operand_batching_dims=(0,),
        start_indices_batching_dims=(0,),
    )
    return lax.gather(
        table,
        index[..., None],
        numbers,
        slice_sizes=(1, 1),
        mode=lax.GatherScatterMode.PROMISE_IN_BOUNDS,
    )


def levels(tables, code):
    numbers = lax.GatherDimensionNumbers(
        offset_dims=(),
        collapsed_slice_dims=(0,),
        start_index_map=(0,),
        operand_batching_dims=(1,),
        start_indices_batching_dims=(1,),
    )

    def pick(table, index):
        return lax.gather(
            table,
            index[..., None],
            numbers,
            slice_sizes=(1, 1),
            mode=lax.GatherScatterMode.PROMISE_IN_BOUNDS,
        )

    parts = []
    for j in range(code.shape[0] // 8):
        part = code[8 * j : 8 * j + 8]
        at = part & 7
        parts.append(jnp.where((part & 8) != 0, pick(tables[1], at), pick(tables[0], at)))
    return jnp.concatenate(parts, axis=0)


def lanes_of(shape):
    return lax.broadcasted_iota(jnp.int32, shape, 1)


def rows_of(shape):
    return lax.broadcasted_iota(jnp.int32, shape, 0)


def dot(a, b):
    return lax.dot_general(a, b, (((1,), (0,)), ((), ())), preferred_element_type=F32)


def dot_nt(a, b):
    return lax.dot_general(a, b, (((1,), (1,)), ((), ())), preferred_element_type=F32)


def two_parts(x):
    high = x.astype(BF16)
    return high, (x - high.astype(F32)).astype(BF16)


def three_parts(x):
    high = x.astype(BF16)
    rest = x - high.astype(F32)
    middle = rest.astype(BF16)
    return [high, middle, (rest - middle.astype(F32)).astype(BF16)]


def even_first():
    row, lane = rows_of((256, 256)), lanes_of((256, 256))
    return jnp.where(row == jnp.where(lane < 128, 2 * lane, 2 * lane - 255), 1.0, 0.0).astype(BF16)


def joined(even, odd):
    n, width = even.shape
    lane = lanes_of((n, 128))
    is_even = (lane & 1) == 0
    blocks = []
    for c in range(width // 64):
        part = slice(128 * (c // 2), 128 * (c // 2) + 128)
        at = 64 * (c % 2) + (lane >> 1)
        blocks.append(jnp.where(is_even, lookup(even[:, part], at), lookup(odd[:, part], at)))
    return blocks


def kernel(
    tenant,
    lengths,
    hidden,
    gain,
    q_codes,
    q_absmax,
    kv_codes,
    kv_absmax,
    o_codes,
    o_absmax,
    q_down,
    q_up,
    q_magnitude,
    o_down,
    o_up,
    o_magnitude,
    pages,
    cache,
    consts,
    out,
    hid_v,
    gain_v,
    qc_v,
    qa_v,
    kc_v,
    ka_v,
    oc_v,
    oa_v,
    qd_v,
    qu_v,
    qm_v,
    od_v,
    ou_v,
    om_v,
    pt_v,
    cache_v,
    const_v,
    ae_v,
    ao_v,
    up_v,
    lhs_v,
    we_v,
    wo_v,
    acc_v,
    sq_v,
    flat_v,
    kvw_v,
    qf_v,
    score_v,
    num_v,
    nbf_v,
    att_v,
    b_src,
    b_dst,
    z_src,
    z_dst,
    c1_src,
    c1_dst,
    c2_dst,
    kv_src,
    kv_dst,
    new_src,
    new_dst,
    n_src,
    n_dst,
    e_src,
    e_dst,
    g_src,
    g_dst,
    load_sem,
    code_sem,
    page_sem,
    bs,
    br,
    zs,
    zr,
    c1s,
    c1r,
    c2s,
    c2r,
    ks,
    kr,
    news,
    newr,
    ns,
    nr,
    es,
    er,
    gs,
    gr,
):
    gx = lax.axis_index("gx")
    gy = lax.axis_index("gy")

    def load(n, src, dst):
        copy = pltpu.make_async_copy(src, dst, load_sem.at[n])
        copy.start()
        return copy

    in_at = pl.multiple_of(gx * LOCAL_IN, LOCAL_IN)
    core = lax.rem(gx, 2)
    partner = gx + 1 - 2 * core
    z = lax.div(gx, 2)
    heads_at = pl.multiple_of(core * HALF, HALF)
    loads = [
        load(0, hidden, hid_v),
        load(1, gain.at[pl.ds(pl.multiple_of(gx * 16, 16), 16), :], gain_v),
        load(2, consts, const_v),
        load(4, q_down, qd_v),
        load(3, q_absmax, qa_v),
        load(5, q_up, qu_v),
    ]
    q_loads = []
    for c in range(CHUNKS):
        part = pl.ds(c * CHUNK, CHUNK)
        q_loads.append(pltpu.make_async_copy(q_codes.at[part, :], qc_v.at[part, :], code_sem.at[c]))
        q_loads[-1].start()
    barrier = pltpu.get_barrier_semaphore()
    for k in range(1, NX):
        pl.semaphore_signal(
            barrier, inc=1, device_id={"gx": lax.rem(gx + k, NX)}, device_id_type=MESH
        )
    for k in range(1, NY):
        pl.semaphore_signal(
            barrier, inc=1, device_id={"gy": lax.rem(gy + k, NY)}, device_id_type=MESH
        )

    def to_partner(src, dst, send, recv):
        return pltpu.make_async_remote_copy(
            src_ref=src,
            dst_ref=dst,
            send_sem=send.at[0],
            recv_sem=recv.at[0],
            device_id={"gx": partner},
            device_id_type=MESH,
        )

    def to_gx(k, src, dst, send, recv):
        return pltpu.make_async_remote_copy(
            src_ref=src,
            dst_ref=dst,
            send_sem=send.at[k],
            recv_sem=recv.at[k],
            device_id={"gx": lax.rem(gx + k, NX)},
            device_id_type=MESH,
        )

    def to_gy(k, src, dst, send, recv):
        return pltpu.make_async_remote_copy(
            src_ref=src,
            dst_ref=dst,
            send_sem=send.at[k],
            recv_sem=recv.at[k],
            device_id={"gy": lax.rem(gy + k, NY)},
            device_id_type=MESH,
        )

    started = []

    row8 = rows_of((ROWS, 128))
    lane8 = lanes_of((ROWS, 128))
    tenant_of = jnp.zeros((ROWS, 128), jnp.int32)
    length_of = jnp.zeros((ROWS, 128), jnp.int32)
    for r in range(ROWS):
        tenant_of = jnp.where(row8 == r, tenant[r], tenant_of)
        length_of = jnp.where(row8 == r, lengths[r], length_of)
    for copy in loads[0:3]:
        copy.wait()
    angles = length_of.astype(F32) * const_v[16:24, :]
    cosine = jnp.cos(angles)
    sine = jnp.sin(angles)
    sine = jnp.where(lane8 < 64, -sine, sine)

    def rope(x):
        return x * cosine + pltpu.roll(x, 64, 1) * sine

    total = jnp.zeros((ROWS, 128), F32)
    for c in range(D // 1024):
        x = hid_v[:, c * 1024 : (c + 1) * 1024].astype(F32)
        x = x * x
        for j in range(8):
            total = total + x[:, j * 128 : (j + 1) * 128]
    inverse = lax.rsqrt(jnp.sum(total, axis=1, keepdims=True) * (1.0 / D) + NORM_EPS)
    states = hid_v[:, pl.ds(in_at, LOCAL_IN)].astype(F32)
    lhs_v[0:16, :] = jnp.zeros((16, LOCAL_IN), BF16)
    normed = []
    for c in range(16):
        x = states[:, c * 128 : (c + 1) * 128] * inverse * gain_v[c : c + 1, :]
        normed.append(x)
    normed = jnp.concatenate(normed, axis=1)
    lhs_v[0:16, :] = jnp.concatenate([normed, jnp.zeros_like(normed)], axis=0).astype(BF16)
    for copy in loads[3:]:
        copy.wait()
    lhs_v[16:144, :] = qd_v[...]

    lane64 = lanes_of((64, 128))
    tables = (const_v[0:8, :], const_v[8:16, :])
    parting = even_first()

    def dequantize(codes, row, scale_row):
        for c in range(4):
            cols = slice(128 * c, 128 * c + 128)
            words = codes[pl.ds(row, 64), cols]
            for half, (scales, ref) in enumerate(((ae_v, we_v), (ao_v, wo_v))):
                code = words & 15 if half == 0 else words >> 4
                value = levels(tables, code) * scales[c, pl.ds(scale_row, 1), :]
                ref[pl.ds(row, 64), cols] = value.astype(BF16)
                square = value * value
                part = square[0:8]
                for j in range(1, 8):
                    part = part + square[8 * j : 8 * j + 8]
                sq_v[half, :, cols] += part

    def weight_chunk(codes, c, lhs_rows):
        base = c * CHUNK
        for b in range(CHUNK // QBLOCK):
            dequantize(codes, base + b * QBLOCK, c * (CHUNK // QBLOCK) + b)
        left = lhs_v[lhs_rows, pl.ds(base, CHUNK)]
        acc_v[0, lhs_rows, :] += dot(left, we_v[pl.ds(base, CHUNK), :])
        acc_v[1, lhs_rows, :] += dot(left, wo_v[pl.ds(base, CHUNK), :])

    def begin_projection(absmax, up):
        for c in range(4):
            part = slice(256 * c, 256 * c + 256)
            parts = dot(jnp.concatenate(three_parts(absmax[:, part]), axis=0), parting)
            whole = parts[0:32] + parts[32:64] + parts[64:96]
            ae_v[c] = whole[:, 0:128]
            ao_v[c] = whole[:, 128:256]
            both = dot(up[:, part], parting).astype(BF16)
            up_v[0, :, 128 * c : 128 * c + 128] = both[:, 0:128]
            up_v[1, :, 128 * c : 128 * c + 128] = both[:, 128:256]
        acc_v[...] = jnp.zeros_like(acc_v)
        sq_v[...] = jnp.zeros_like(sq_v)

    def norm_parts(gram):
        same = (rows_of((128, 128)) >> 4) == (lanes_of((128, 128)) >> 4)
        high, low = two_parts(jnp.where(same, gram, 0.0))
        halves = []
        for half in range(2):
            up = up_v[half]
            inner = 2.0 * acc_v[half, 16:144, :] + (dot(high, up) + dot(low, up))
            terms = jnp.sum((up.astype(F32) * inner).reshape(TENANTS, RANK, HALF), axis=1)
            terms = terms + jnp.sum(sq_v[half], axis=0, keepdims=True)
            mine = tenant_of[:, 0:1]
            chosen = jnp.zeros((ROWS, HALF), F32)
            for t in range(TENANTS):
                chosen = jnp.where(mine == t, terms[t : t + 1, :], chosen)
            halves.append(chosen)
        return halves

    def adapter(middle):
        masked = jnp.where(tenant_of == (lane8 >> 4), middle, 0.0)
        high = masked.astype(BF16).astype(F32)
        both = jnp.concatenate([high, masked - high], axis=0).astype(BF16)
        halves = []
        for half in range(2):
            x = dot(both, up_v[half])
            halves.append(x[0:8] + x[8:16])
        return halves


    begin_projection(qa_v, qu_v)

    inner = dot_nt(lhs_v[...], lhs_v[16:144, :])
    middle, gram = inner[0:8], inner[16:144]

    for c in range(CHUNKS):
        q_loads[c].wait()
        if c == LATER:
            later = [
                load(6, kv_codes, kc_v),
                load(7, kv_absmax, ka_v),
                load(8, q_magnitude.at[:, pl.ds(heads_at, HALF)], qm_v),
                load(9, pages, pt_v),
            ]
            o_small = [load(10, o_absmax, oa_v), load(11, o_down, od_v), load(12, o_up, ou_v), load(13, o_magnitude, om_v)]
            o_loads = [pltpu.make_async_copy(o_codes, oc_v, code_sem.at[CHUNKS])]
            o_loads[0].start()
            page_loads = []
            for s in range(SLOTS):
                page_loads.append(pltpu.make_async_copy(cache.at[s], cache_v.at[s], page_sem.at[s]))
                page_loads[-1].start()

        weight_chunk(qc_v, c, slice(0, 144))

    extra = adapter(middle)
    product = joined(acc_v[0, 0:8, :] + extra[0], acc_v[1, 0:8, :] + extra[1])
    norms = joined(*norm_parts(gram))
    for half in range(2):
        for m in range(4):
            b_src[half, m] = product[4 * half + m]
            b_src[half, 4 + m] = norms[4 * half + m]

    pl.semaphore_wait(barrier, NX - 1 + NY - 1)

    b_copy = to_partner(b_src.at[1 - core], b_dst, bs, br)
    b_copy.start()
    started.append(b_copy)
    for copy in o_small:
        copy.wait()
    lhs_v[16:144, :] = od_v[...]
    o_gram = dot_nt(lhs_v[16:144, :], lhs_v[16:144, :])
    b_copy.wait_recv()
    z_src[...] = b_src[core] + b_dst[...]
    z_dst[z] = z_src[...]
    z_copies = []
    for k in range(1, 4):
        z_copies.append(to_gx(2 * k, z_src, z_dst.at[z], zs, zr))
        z_copies[-1].start()
    started += z_copies

    for copy in later:
        copy.wait()
    lane32 = lanes_of((32, 128))
    at = jnp.where(lane32 < 64, 2 * lane32, 2 * lane32 - 127)
    kv_scale = jnp.concatenate(
        [lookup(ka_v[...], at), jnp.zeros((96, 128), F32)], axis=0
    ).T
    for c in range(16):
        words = kc_v[:, c * 128 : (c + 1) * 128]
        for half in range(2):
            code = words & 15 if half == 0 else words >> 4
            scale = lookup(kv_scale[64 * half : 64 * half + 64], 2 * c + (lane64 >> 6))
            kvw_v[64 * half : 64 * half + 64, c * 128 : (c + 1) * 128] = (
                levels(tables, code) * scale
            ).astype(BF16)
    keyval = dot_nt(lhs_v[0:16, :], kvw_v[...])[0:8]
    keyval = lookup(keyval, jnp.where((lane8 & 1) == 0, lane8 >> 1, 64 + (lane8 >> 1)))

    kv_src[...] = keyval
    kv_copies = []
    for k in range(1, NX):
        kv_copies.append(to_gx(k, kv_src, kv_dst.at[k], ks, kr))
        kv_copies[-1].start()
    started += kv_copies
    begin_projection(oa_v, ou_v)
    for copy in o_loads:
        copy.wait()
    down_rows = slice(16, 144)
    for c in range(FIRST):
        weight_chunk(oc_v, c, down_rows)

    for copy in z_copies:
        copy.wait_recv()
    summed = z_dst[0]
    for k in range(1, 4):
        summed = summed + z_dst[k]
    queries = []
    for m in range(4):
        magnitude = jnp.zeros((ROWS, 128), F32)
        for t in range(TENANTS):
            magnitude = jnp.where(
                tenant_of == t, qm_v[t : t + 1, 128 * m : 128 * m + 128], magnitude
            )
        queries.append(rope(summed[m] * (magnitude * lax.rsqrt(summed[4 + m]))))
    c1_src[0:16, :] = jnp.concatenate(queries[0:2], axis=0).astype(BF16)
    c1_src[16:32, :] = jnp.concatenate(queries[2:4], axis=0).astype(BF16)
    c1_dst[gy] = c1_src[...]
    c1_copies = []
    for k in range(1, NY):
        c1_copies.append(to_gy(k, c1_src, c1_dst.at[gy], c1s, c1r))
        c1_copies[-1].start()
    started += c1_copies
    for copy in kv_copies:
        copy.wait_recv()
    new = kv_src[...]
    for k in range(1, NX):
        new = new + kv_dst[k]
    new = jnp.where(gy < KV_HEADS, rope(new), new)
    new_src[...] = jnp.concatenate([new, jnp.zeros_like(new)], axis=0).astype(BF16)
    new_dst[gy] = new_src[...]
    new_copies = []
    for k in range(1, NY):
        new_copies.append(to_gy(k, new_src, new_dst.at[gy], news, newr))
        new_copies[-1].start()
    started += new_copies
    for c in range(FIRST, CHUNKS):
        weight_chunk(oc_v, c, down_rows)
    o_norms = joined(*norm_parts(o_gram))
    for i in range(8):
        flat_v[8 * i : 8 * i + 8, :] = o_norms[i]
    for r in range(ROWS):
        g_src[r, 1] = flat_v[pl.ds(r, 8, stride=8), :]

    page_no = lanes_of((ROWS, 96))
    row_no = rows_of((ROWS, 96))
    length = length_of[:, 0:96]
    live = page_no * PAGE < length
    remaining = jnp.clip(length - page_no * PAGE, 0, PAGE)
    table_pages = pt_v[...]

    def whole(x):
        return jnp.sum(jnp.sum(x.astype(F32), axis=1, keepdims=True), axis=0, keepdims=True)

    owner, filled = [], []
    for s in range(SLOTS):
        hit = jnp.logical_and(table_pages == (gx * NY + gy) * SLOTS + s, live)
        owner.append(whole(jnp.where(hit, row_no, 0)))
        filled.append(whole(jnp.where(hit, remaining, 0)))

    def same(a, b):
        return jnp.where(a == b, 1.0, 0.0).astype(F32)

    for copy in c1_copies:
        copy.wait_recv()
    c2_copy = to_partner(c1_dst, c2_dst, c2s, c2r)
    c2_copy.start()
    started.append(c2_copy)
    for j in range(NY):
        block = c1_dst[j].astype(F32)
        for m in range(4):
            qf_v[pl.ds(8 * j + 4 * core + m, 8, stride=HEADS), :] = block[8 * m : 8 * m + 8]
    c2_copy.wait_recv()
    for j in range(NY):
        block = c2_dst[j].astype(F32)
        for m in range(4):
            qf_v[pl.ds(8 * j + 4 - 4 * core + m, 8, stride=HEADS), :] = block[8 * m : 8 * m + 8]

    even_group = ((rows_of((HEADS, 128)) >> 4) & 1) == 0
    token = lanes_of((HEADS, PAGE)).astype(F32)
    peaks = []
    for s in range(SLOTS):
        q = jnp.zeros((HEADS, HEAD_DIM), F32)
        for r in range(ROWS):
            q = q + qf_v[r * HEADS : (r + 1) * HEADS, :] * same(owner[s], float(r))
        q = jnp.concatenate(
            [jnp.where(even_group, q, 0.0), jnp.where(even_group, 0.0, q)], axis=1
        ).astype(BF16)
        page_loads[s].wait()
        parts = [
            dot_nt(q[32 * p : 32 * p + 32], cache_v[s, 0, :, 256 * p : 256 * p + 256])
            for p in range(4)
        ]
        score = jnp.concatenate(parts, axis=0) * INV_ROOT
        score = jnp.where(token < filled[s], score, NEG_FILL)
        score_v[s] = score
        peaks.append(jnp.max(score, axis=1, keepdims=True))
    totals = []
    for s in range(SLOTS):
        peak = peaks[s]
        for other in range(SLOTS):
            if other != s:
                alike = owner[s] == owner[other]
                peak = jnp.maximum(peak, jnp.where(alike, peaks[other], NEG_FILL))
        weights = jnp.where(token < filled[s], jnp.exp(score_v[s] - peak), 0.0).astype(BF16)
        totals.append(jnp.sum(weights.astype(F32), axis=1, keepdims=True))
        for p in range(4):
            x = dot(weights[32 * p : 32 * p + 32], cache_v[s, 1, :, 256 * p : 256 * p + 256])
            num_v[s, 32 * p : 32 * p + 16, :] = x[0:16, 0:128]
            num_v[s, 32 * p + 16 : 32 * p + 32, :] = x[16:32, 128:256]
    lane_h = lanes_of((HEADS, 128))
    stats = jnp.zeros((HEADS, 128), F32)
    for r in range(ROWS):
        number = jnp.zeros((HEADS, HEAD_DIM), F32)
        peak = jnp.full((HEADS, 1), NEG_FILL, F32)
        total = jnp.zeros((HEADS, 1), F32)
        for s in range(SLOTS):
            mine = same(owner[s], float(r))
            number = number + num_v[s] * mine
            total = total + totals[s] * mine
            peak = jnp.maximum(peak, jnp.where(owner[s] == float(r), peaks[s], NEG_FILL))
        nbf_v[pl.ds(r, HEADS, stride=ROWS), :] = number
        stats = jnp.where(lane_h == r, peak, stats)
        stats = jnp.where(lane_h == 8 + r, total, stats)
    stats = three_parts(stats.T[0:16])
    stats = [x.astype(F32) for x in stats]
    lane16 = lanes_of((16, 128))
    for i in range(NX):
        n_src[i, 0:128, :] = nbf_v[128 * i : 128 * i + 128, :].astype(BF16)
        mine = [pltpu.roll(x, (16 * n - 16 * i) % 128, 1) if (n - i) % 8 else x for n, x in enumerate(stats)]
        n_src[i, 128:144, :] = jnp.where(
            lane16 < 16, mine[0], jnp.where(lane16 < 32, mine[1], mine[2])
        ).astype(BF16)

    n_copies = []
    for k in range(1, NX):
        peer = lax.rem(gx + k, NX)
        n_copies.append(to_gx(k, n_src.at[peer], n_dst.at[k], ns, nr))
        n_copies[-1].start()
    started += n_copies

    for copy in new_copies:
        copy.wait_recv()
    new_key = new_dst[gx].astype(F32)[0:8]
    new_value = new_dst[KV_HEADS + gx].astype(F32)[0:8]
    self_score = jnp.zeros((ROWS, 128), F32)
    for h in range(16):
        q = qf_v[pl.ds(16 * gx + h, 8, stride=HEADS), :]
        score = jnp.sum(q * new_key, axis=1, keepdims=True) * INV_ROOT
        self_score = jnp.where(lane8 == h, score, self_score)

    states = hid_v[:, pl.ds(pl.multiple_of(gy * 1024, 1024), 1024)].astype(F32)
    mine = tenant[gx]
    out_magnitude = jnp.zeros((8, 128), F32)
    for i in range(8):
        flat_v[8 * i : 8 * i + 8, :] = om_v[:, 128 * i : 128 * i + 128]
    for t in range(TENANTS):
        out_magnitude = jnp.where(mine == t, flat_v[pl.ds(t, 8, stride=8), :], out_magnitude)
    for i in range(8):
        flat_v[8 * i : 8 * i + 8, :] = states[:, 128 * i : 128 * i + 128]
    residual = flat_v[pl.ds(gx, 8, stride=8), :]

    def gathered(x, first):
        parts = [pltpu.roll(x, 128 - first - 16 * n, 1) if first + n else x for n in range(3)]
        return parts[0] + parts[1] + parts[2]

    for copy in n_copies:
        copy.wait_recv()
    n_dst[0] = n_src[gx]
    seen = [gathered(n_dst[k, 128:144, :].astype(F32), 0) for k in range(NX)]
    peak = seen[0][0:8]
    for k in range(1, NX):
        peak = jnp.maximum(peak, seen[k][0:8])
    total = jnp.zeros((ROWS, 128), F32)
    factors = []
    for k in range(NX):
        factors.append(jnp.exp(seen[k][0:8] - peak))
        total = total + factors[k] * seen[k][8:16]
    for j in range(8):
        pair = [jnp.zeros((ROWS, 128), F32), jnp.zeros((ROWS, 128), F32)]
        for k in range(NX):
            block = n_dst[k, 16 * j : 16 * j + 16, :].astype(F32)
            for n in range(2):
                h = 2 * j + n
                pair[n] = pair[n] + block[8 * n : 8 * n + 8] * factors[k][:, h : h + 1]
        e_src[16 * j : 16 * j + 16, :] = jnp.concatenate(pair, axis=0).astype(BF16)
    stats = jnp.zeros((ROWS, 128), F32)
    for n, x in enumerate(three_parts(peak) + three_parts(total)):
        x = x.astype(F32)
        x = pltpu.roll(x, 16 * n, 1) if n else x
        stats = jnp.where(jnp.logical_and(lane8 >= 16 * n, lane8 < 16 * n + 16), x, stats)
    e_src[128:144, :] = jnp.concatenate([stats, jnp.zeros_like(stats)], axis=0).astype(BF16)

    e_dst[gy] = e_src[...]
    e_copies = []
    for k in range(1, NY):
        e_copies.append(to_gy(k, e_src, e_dst.at[gy], es, er))
        e_copies[-1].start()
    started += e_copies
    for copy in e_copies:
        copy.wait_recv()
    peaks, totals = [], []
    peak = self_score
    for k in range(NY):
        x = e_dst[k, 128:144, :].astype(F32)[0:8]
        peaks.append(gathered(x, 0))
        totals.append(gathered(x, 48))
        peak = jnp.maximum(peak, peaks[k])
    own = jnp.exp(self_score - peak)
    total = own
    factors = []
    for k in range(NY):
        factors.append(jnp.exp(peaks[k] - peak))
        total = total + factors[k] * totals[k]
    for j in range(8):
        pair = [own[:, 2 * j + n : 2 * j + n + 1] * new_value for n in range(2)]
        for k in range(NY):
            block = e_dst[k, 16 * j : 16 * j + 16, :].astype(F32)
            for n in range(2):
                h = 2 * j + n
                pair[n] = pair[n] + block[8 * n : 8 * n + 8] * factors[k][:, h : h + 1]
        for n in range(2):
            h = 2 * j + n
            x = pair[n] / total[:, h : h + 1]
            att_v[:, 128 * h : 128 * h + 128] = jnp.concatenate([x, jnp.zeros_like(x)], axis=0).astype(BF16)

    attended = att_v[...]
    middle = dot_nt(attended, lhs_v[16:144, :])[0:8]
    extra = adapter(middle)
    projected = joined(
        dot(attended, we_v[...])[0:8] + extra[0], dot(attended, wo_v[...])[0:8] + extra[1]
    )
    for i in range(8):
        flat_v[8 * i : 8 * i + 8, :] = projected[i]
    for r in range(ROWS):
        g_src[r, 0] = flat_v[pl.ds(r, 8, stride=8), :]
    g_copies = []
    for k in range(1, NX):
        peer = lax.rem(gx + k, NX)
        g_copies.append(to_gx(k, g_src.at[peer], g_dst.at[k], gs, gr))
        g_copies[-1].start()
    started += g_copies

    summed = [g_src[gx, j] for j in range(2)]
    for copy in g_copies:
        copy.wait_recv()
    for k in range(1, NX):
        for j in range(2):
            summed[j] = summed[j] + g_dst[k, j]
    result = (residual + summed[0] * (out_magnitude * lax.rsqrt(summed[1])))
    for c in range(8):
        out[0:1, 128 * c : 128 * c + 128] = result[c : c + 1, :]
    for copy in started:
        copy.wait_send()


def local(
    hidden,
    norm_gain,
    q_codes,
    q_absmax,
    kv_codes,
    kv_absmax,
    o_codes,
    o_absmax,
    q_down,
    q_up,
    q_magnitude,
    o_down,
    o_up,
    o_magnitude,
    tenant,
    lengths,
    page_table,
    kv_cache,
):
    def down_rows(down):
        return jnp.transpose(down, (0, 2, 1)).reshape(TENANTS * RANK, LOCAL_IN)

    def up_rows(up):
        return up.reshape(TENANTS * RANK, 1024)

    vmem = pltpu.VMEM
    dma = pltpu.SemaphoreType.DMA
    hbm = pl.BlockSpec(memory_space=pl.ANY)
    smem = pl.BlockSpec(memory_space=pltpu.SMEM)
    scratch = [
        vmem((8, D), BF16),
        vmem((16, 128), F32),
        vmem((LOCAL_IN, HALF), jnp.int32),
        vmem((32, 1024), F32),
        vmem((64, LOCAL_IN), jnp.int32),
        vmem((32, 128), F32),
        vmem((LOCAL_IN, HALF), jnp.int32),
        vmem((32, 1024), F32),
        vmem((128, LOCAL_IN), BF16),
        vmem((128, 1024), BF16),
        vmem((8, HALF), F32),
        vmem((128, LOCAL_IN), BF16),
        vmem((128, 1024), BF16),
        vmem((8, 1024), F32),
        vmem((8, 96), jnp.int32),
        vmem((SLOTS, 2, PAGE, 1024), BF16),
        vmem((24, 128), F32),
        vmem((4, 32, 128), F32),
        vmem((4, 32, 128), F32),
        vmem((2, 128, HALF), BF16),
        vmem((144, LOCAL_IN), BF16),
        vmem((LOCAL_IN, HALF), BF16),
        vmem((LOCAL_IN, HALF), BF16),
        vmem((2, 144, HALF), F32),
        vmem((2, 8, HALF), F32),
        vmem((64, 128), F32),
        vmem((128, LOCAL_IN), BF16),
        vmem((ROWS * HEADS, HEAD_DIM), F32),
        vmem((SLOTS, HEADS, PAGE), F32),
        vmem((SLOTS, HEADS, HEAD_DIM), F32),
        vmem((ROWS * HEADS, HEAD_DIM), F32),
        vmem((16, LOCAL_IN), BF16),
        vmem((2, 8, 8, 128), F32),
        vmem((8, 8, 128), F32),
        vmem((8, 8, 128), F32),
        vmem((4, 8, 8, 128), F32),
        vmem((32, 128), BF16),
        vmem((NY, 32, 128), BF16),
        vmem((NY, 32, 128), BF16),
        vmem((8, 128), F32),
        vmem((NX, 8, 128), F32),
        vmem((16, 128), BF16),
        vmem((NY, 16, 128), BF16),
        vmem((NX, 144, 128), BF16),
        vmem((NX, 144, 128), BF16),
        vmem((144, 128), BF16),
        vmem((NY, 144, 128), BF16),
        vmem((NX, 2, 8, 128), F32),
        vmem((NX, 2, 8, 128), F32),
        dma((14,)),
        dma((CHUNKS + 1,)),
        dma((SLOTS,)),
        dma((1,)),
        dma((1,)),
        dma((NX,)),
        dma((NX,)),
        dma((NY,)),
        dma((NY,)),
        dma((1,)),
        dma((1,)),
        dma((NX,)),
        dma((NX,)),
        dma((NY,)),
        dma((NY,)),
        dma((NX,)),
        dma((NX,)),
        dma((NY,)),
        dma((NY,)),
        dma((NX,)),
        dma((NX,)),
    ]
    result = pl.pallas_call(
        kernel,
        out_shape=jax.ShapeDtypeStruct((1, 1024), F32),
        in_specs=[smem, smem] + [hbm] * 17,
        out_specs=pl.BlockSpec(memory_space=pltpu.VMEM),
        scratch_shapes=scratch,
        compiler_params=pltpu.CompilerParams(
            collective_id=0, has_side_effects=True, vmem_limit_bytes=56 * 1024 * 1024
        ),
        name="layer",
    )(
        tenant,
        lengths,
        hidden,
        norm_gain.reshape(128, 128),
        q_codes,
        q_absmax,
        kv_codes.T,
        kv_absmax,
        o_codes,
        o_absmax,
        down_rows(q_down),
        up_rows(q_up),
        q_magnitude,
        down_rows(o_down),
        up_rows(o_up),
        o_magnitude,
        page_table,
        kv_cache,
        jnp.asarray(constants()),
    )
    return result.astype(BF16)


def solution(mesh):
    in_specs = (
        P(),
        P(),
        P("gx", "gy"),
        P("gx", "gy"),
        P("gx", "gy"),
        P("gx", "gy"),
        P("gx", "gy"),
        P("gx", "gy"),
        P(None, "gx", None),
        P(None, None, "gy"),
        P(None, "gy"),
        P(None, "gx", None),
        P(None, None, "gy"),
        P(None, "gy"),
        P(),
        P(),
        P(),
        P(("gx", "gy"), None, None, None),
    )
    return jax.shard_map(
        local, mesh=mesh, in_specs=in_specs, out_specs=P("gx", "gy"), check_vma=False
    )
```

```python
import functools
import math

import jax
import jax.numpy as jnp
import numpy as np
from jax import lax
from jax.experimental import pallas as pl
from jax.experimental.pallas import tpu as pltpu
from jax.sharding import PartitionSpec as P

HEADS = 128
KV_HEADS = 8
HEAD_DIM = 128
TENANTS = 8
RANK = 16
QBLOCK = 64
PAGE = 256
ROWS = 8
NX = 8
NY = 16
SLOTS = 5
LOCAL_IN = 2048
HALF = 512
CHUNK = 256
CHUNKS = LOCAL_IN // CHUNK
LATER = 5
FIRST = 2
D = 16384

NF4_LEVELS = (
    -1.0,
    -0.6961928009986877,
    -0.5250730514526367,
    -0.39491748809814453,
    -0.28444138169288635,
    -0.18477343022823334,
    -0.09105003625154495,
    0.0,
    0.07958029955625534,
    0.16093020141124725,
    0.24611230194568634,
    0.33791524171829224,
    0.44070982933044434,
    0.5626170039176941,
    0.7229568362236023,
    1.0,
)
NORM_EPS = 1e-05
NEG_FILL = -1e30
ROPE_BASE = 500000.0
MESH = pl.DeviceIdType.MESH
F32 = jnp.float32
BF16 = jnp.bfloat16
INV_ROOT = 1.0 / math.sqrt(HEAD_DIM)


def constants():
    table = np.zeros((24, 128), np.float32)
    table[:16] = np.asarray(NF4_LEVELS, np.float32)[:, None]
    frequency = ROPE_BASE ** (-2.0 * np.arange(64, dtype=np.float64) / HEAD_DIM)
    table[16:] = np.concatenate([frequency, frequency]).astype(np.float32)[None]
    return table


def lookup(table, index):
    numbers = lax.GatherDimensionNumbers(
        offset_dims=(),
        collapsed_slice_dims=(1,),
        start_index_map=(1,),
        operand_batching_dims=(0,),
        start_indices_batching_dims=(0,),
    )
    return lax.gather(
        table,
        index[..., None],
        numbers,
        slice_sizes=(1, 1),
        mode=lax.GatherScatterMode.PROMISE_IN_BOUNDS,
    )


def levels(tables, words, high):
    numbers = lax.GatherDimensionNumbers(
        offset_dims=(),
        collapsed_slice_dims=(0,),
        start_index_map=(0,),
        operand_batching_dims=(1,),
        start_indices_batching_dims=(1,),
    )

    def pick(table, index):
        return lax.gather(
            table,
            index[..., None],
            numbers,
            slice_sizes=(1, 1),
            mode=lax.GatherScatterMode.PROMISE_IN_BOUNDS,
        )

    parts = []
    for j in range(words.shape[0] // 8):
        part = words[8 * j : 8 * j + 8]
        at = (part >> 4 if high else part) & 7
        upper = part > 127 if high else (part & 8) != 0
        parts.append(jnp.where(upper, pick(tables[1], at), pick(tables[0], at)))
    return jnp.concatenate(parts, axis=0)


def lanes_of(shape):
    return lax.broadcasted_iota(jnp.int32, shape, 1)


def rows_of(shape):
    return lax.broadcasted_iota(jnp.int32, shape, 0)


def dot(a, b):
    return lax.dot_general(a, b, (((1,), (0,)), ((), ())), preferred_element_type=F32)


def dot_nt(a, b):
    return lax.dot_general(a, b, (((1,), (1,)), ((), ())), preferred_element_type=F32)


def two_parts(x):
    high = x.astype(BF16)
    return high, (x - high.astype(F32)).astype(BF16)


def three_parts(x):
    high = x.astype(BF16)
    rest = x - high.astype(F32)
    middle = rest.astype(BF16)
    return [high, middle, (rest - middle.astype(F32)).astype(BF16)]


def even_first():
    row, lane = rows_of((256, 256)), lanes_of((256, 256))
    return jnp.where(row == jnp.where(lane < 128, 2 * lane, 2 * lane - 255), 1.0, 0.0).astype(BF16)


def joined(even, odd):
    n, width = even.shape
    lane = lanes_of((n, 128))
    is_even = (lane & 1) == 0
    blocks = []
    for c in range(width // 64):
        part = slice(128 * (c // 2), 128 * (c // 2) + 128)
        at = 64 * (c % 2) + (lane >> 1)
        blocks.append(jnp.where(is_even, lookup(even[:, part], at), lookup(odd[:, part], at)))
    return blocks


def kernel(
    tenant_h,
    lengths_h,
    hidden,
    gain,
    q_codes,
    q_absmax,
    kv_codes,
    kv_absmax,
    o_codes,
    o_absmax,
    q_down,
    q_up,
    q_magnitude,
    o_down,
    o_up,
    o_magnitude,
    pages,
    cache,
    consts,
    out,
    tenant,
    lengths,
    hid_v,
    gain_v,
    qc_v,
    qa_v,
    kc_v,
    ka_v,
    oc_v,
    oa_v,
    qd_v,
    qu_v,
    qm_v,
    od_v,
    ou_v,
    om_v,
    pt_v,
    cache_v,
    const_v,
    ae_v,
    ao_v,
    up_v,
    lhs_v,
    we_v,
    wo_v,
    acc_v,
    sq_v,
    flat_v,
    kvw_v,
    qf_v,
    score_v,
    num_v,
    nbf_v,
    att_v,
    b_src,
    b_dst,
    z_src,
    z_dst,
    c1_src,
    c1_dst,
    c2_dst,
    kv_src,
    kv_dst,
    new_src,
    new_dst,
    n_src,
    n_dst,
    e_src,
    e_dst,
    g_src,
    g_dst,
    load_sem,
    code_sem,
    page_sem,
    bs,
    br,
    zs,
    zr,
    c1s,
    c1r,
    c2s,
    c2r,
    ks,
    kr,
    news,
    newr,
    ns,
    nr,
    es,
    er,
    gs,
    gr,
):
    gx = lax.axis_index("gx")
    gy = lax.axis_index("gy")

    def load(n, src, dst):
        copy = pltpu.make_async_copy(src, dst, load_sem.at[n])
        copy.start()
        return copy

    in_at = pl.multiple_of(gx * LOCAL_IN, LOCAL_IN)
    core = lax.rem(gx, 2)
    partner = gx + 1 - 2 * core
    z = lax.div(gx, 2)
    heads_at = pl.multiple_of(core * HALF, HALF)
    loads = [
        load(14, tenant_h, tenant),
        load(15, lengths_h, lengths),
        load(0, hidden, hid_v),
        load(1, gain.at[pl.ds(pl.multiple_of(gx * 16, 16), 16), :], gain_v),
        load(2, consts, const_v),
        load(4, q_down, qd_v),
        load(3, q_absmax, qa_v),
        load(5, q_up, qu_v),
    ]
    q_loads = []
    for c in range(CHUNKS):
        part = pl.ds(c * CHUNK, CHUNK)
        q_loads.append(pltpu.make_async_copy(q_codes.at[part, :], qc_v.at[part, :], code_sem.at[c]))
        q_loads[-1].start()
    barrier = pltpu.get_barrier_semaphore()
    for k in range(1, NX):
        pl.semaphore_signal(
            barrier, inc=1, device_id={"gx": lax.rem(gx + k, NX)}, device_id_type=MESH
        )
    for k in range(1, NY):
        pl.semaphore_signal(
            barrier, inc=1, device_id={"gy": lax.rem(gy + k, NY)}, device_id_type=MESH
        )

    def to_partner(src, dst, send, recv):
        return pltpu.make_async_remote_copy(
            src_ref=src,
            dst_ref=dst,
            send_sem=send.at[0],
            recv_sem=recv.at[0],
            device_id={"gx": partner},
            device_id_type=MESH,
        )

    def to_gx(k, src, dst, send, recv):
        return pltpu.make_async_remote_copy(
            src_ref=src,
            dst_ref=dst,
            send_sem=send.at[k],
            recv_sem=recv.at[k],
            device_id={"gx": lax.rem(gx + k, NX)},
            device_id_type=MESH,
        )

    def to_gy(k, src, dst, send, recv):
        return pltpu.make_async_remote_copy(
            src_ref=src,
            dst_ref=dst,
            send_sem=send.at[k],
            recv_sem=recv.at[k],
            device_id={"gy": lax.rem(gy + k, NY)},
            device_id_type=MESH,
        )

    started = []

    for copy in loads[0:5]:
        copy.wait()

    row8 = rows_of((ROWS, 128))
    lane8 = lanes_of((ROWS, 128))
    tenant_of = jnp.zeros((ROWS, 128), jnp.int32)
    length_of = jnp.zeros((ROWS, 128), jnp.int32)
    for r in range(ROWS):
        tenant_of = jnp.where(row8 == r, tenant[r], tenant_of)
        length_of = jnp.where(row8 == r, lengths[r], length_of)
    angles = length_of.astype(F32) * const_v[16:24, :]
    cosine = jnp.cos(angles)
    sine = jnp.sin(angles)
    sine = jnp.where(lane8 < 64, -sine, sine)

    def rope(x):
        return x * cosine + pltpu.roll(x, 64, 1) * sine

    total = jnp.zeros((ROWS, 128), F32)
    for c in range(D // 1024):
        x = hid_v[:, c * 1024 : (c + 1) * 1024].astype(F32)
        x = x * x
        for j in range(8):
            total = total + x[:, j * 128 : (j + 1) * 128]
    inverse = lax.rsqrt(jnp.sum(total, axis=1, keepdims=True) * (1.0 / D) + NORM_EPS)
    states = hid_v[:, pl.ds(in_at, LOCAL_IN)].astype(F32)
    lhs_v[0:16, :] = jnp.zeros((16, LOCAL_IN), BF16)
    normed = []
    for c in range(16):
        x = states[:, c * 128 : (c + 1) * 128] * inverse * gain_v[c : c + 1, :]
        normed.append(x)
    normed = jnp.concatenate(normed, axis=1)
    lhs_v[0:16, :] = jnp.concatenate([normed, jnp.zeros_like(normed)], axis=0).astype(BF16)
    for copy in loads[5:]:
        copy.wait()
    lhs_v[16:144, :] = qd_v[...]

    lane64 = lanes_of((64, 128))
    tables = (const_v[0:8, :], const_v[8:16, :])
    parting = even_first()

    def dequantize(codes, row, scale_row):
        for c in range(4):
            cols = slice(128 * c, 128 * c + 128)
            words = codes[pl.ds(row, 64), cols]
            for half, (scales, ref) in enumerate(((ae_v, we_v), (ao_v, wo_v))):
                value = levels(tables, words, half == 1) * scales[c, pl.ds(scale_row, 1), :]
                ref[pl.ds(row, 64), cols] = value.astype(BF16)
                square = value * value
                part = square[0:8]
                for j in range(1, 8):
                    part = part + square[8 * j : 8 * j + 8]
                sq_v[half, :, cols] += part

    def weight_chunk(codes, c, lhs_rows):
        base = c * CHUNK
        for b in range(CHUNK // QBLOCK):
            dequantize(codes, base + b * QBLOCK, c * (CHUNK // QBLOCK) + b)
        left = lhs_v[lhs_rows, pl.ds(base, CHUNK)]
        acc_v[0, lhs_rows, :] += dot(left, we_v[pl.ds(base, CHUNK), :])
        acc_v[1, lhs_rows, :] += dot(left, wo_v[pl.ds(base, CHUNK), :])

    def begin_projection(absmax, up):
        for c in range(4):
            part = slice(256 * c, 256 * c + 256)
            parts = dot(jnp.concatenate(three_parts(absmax[:, part]), axis=0), parting)
            whole = parts[0:32] + parts[32:64] + parts[64:96]
            ae_v[c] = whole[:, 0:128]
            ao_v[c] = whole[:, 128:256]
            both = dot(up[:, part], parting).astype(BF16)
            up_v[0, :, 128 * c : 128 * c + 128] = both[:, 0:128]
            up_v[1, :, 128 * c : 128 * c + 128] = both[:, 128:256]
        acc_v[...] = jnp.zeros_like(acc_v)
        sq_v[...] = jnp.zeros_like(sq_v)

    def norm_parts(gram):
        same = (rows_of((128, 128)) >> 4) == (lanes_of((128, 128)) >> 4)
        high, low = two_parts(jnp.where(same, gram, 0.0))
        halves = []
        for half in range(2):
            up = up_v[half]
            inner = 2.0 * acc_v[half, 16:144, :] + (dot(high, up) + dot(low, up))
            terms = jnp.sum((up.astype(F32) * inner).reshape(TENANTS, RANK, HALF), axis=1)
            terms = terms + jnp.sum(sq_v[half], axis=0, keepdims=True)
            mine = tenant_of[:, 0:1]
            chosen = jnp.zeros((ROWS, HALF), F32)
            for t in range(TENANTS):
                chosen = jnp.where(mine == t, terms[t : t + 1, :], chosen)
            halves.append(chosen)
        return halves

    def adapter(middle):
        masked = jnp.where(tenant_of == (lane8 >> 4), middle, 0.0)
        high = masked.astype(BF16).astype(F32)
        both = jnp.concatenate([high, masked - high], axis=0).astype(BF16)
        halves = []
        for half in range(2):
            x = dot(both, up_v[half])
            halves.append(x[0:8] + x[8:16])
        return halves


    begin_projection(qa_v, qu_v)

    inner = dot_nt(lhs_v[...], lhs_v[16:144, :])
    middle, gram = inner[0:8], inner[16:144]

    for c in range(CHUNKS):
        q_loads[c].wait()
        if c == LATER:
            later = [
                load(6, kv_codes, kc_v),
                load(7, kv_absmax, ka_v),
                load(8, q_magnitude.at[:, pl.ds(heads_at, HALF)], qm_v),
                load(9, pages, pt_v),
            ]
            o_small = [load(10, o_absmax, oa_v), load(11, o_down, od_v), load(12, o_up, ou_v), load(13, o_magnitude, om_v)]
            o_loads = [pltpu.make_async_copy(o_codes, oc_v, code_sem.at[CHUNKS])]
            o_loads[0].start()
            page_loads = []
            for s in range(SLOTS):
                page_loads.append(pltpu.make_async_copy(cache.at[s], cache_v.at[s], page_sem.at[s]))
                page_loads[-1].start()

        weight_chunk(qc_v, c, slice(0, 144))

    extra = adapter(middle)
    product = joined(acc_v[0, 0:8, :] + extra[0], acc_v[1, 0:8, :] + extra[1])
    norms = joined(*norm_parts(gram))
    for half in range(2):
        for m in range(4):
            b_src[half, m] = product[4 * half + m]
            b_src[half, 4 + m] = norms[4 * half + m]

    pl.semaphore_wait(barrier, NX - 1 + NY - 1)

    b_copy = to_partner(b_src.at[1 - core], b_dst, bs, br)
    b_copy.start()
    started.append(b_copy)
    for copy in o_small:
        copy.wait()
    lhs_v[16:144, :] = od_v[...]
    o_gram = dot_nt(lhs_v[16:144, :], lhs_v[16:144, :])
    b_copy.wait_recv()
    z_src[...] = b_src[core] + b_dst[...]
    z_dst[z] = z_src[...]
    z_copies = []
    for k in range(1, 4):
        z_copies.append(to_gx(2 * k, z_src, z_dst.at[z], zs, zr))
        z_copies[-1].start()
    started += z_copies

    for copy in later:
        copy.wait()
    lane32 = lanes_of((32, 128))
    at = jnp.where(lane32 < 64, 2 * lane32, 2 * lane32 - 127)
    kv_scale = jnp.concatenate(
        [lookup(ka_v[...], at), jnp.zeros((96, 128), F32)], axis=0
    ).T
    for c in range(16):
        words = kc_v[:, c * 128 : (c + 1) * 128]
        for half in range(2):
            scale = lookup(kv_scale[64 * half : 64 * half + 64], 2 * c + (lane64 >> 6))
            kvw_v[64 * half : 64 * half + 64, c * 128 : (c + 1) * 128] = (
                levels(tables, words, half == 1) * scale
            ).astype(BF16)
    keyval = dot_nt(lhs_v[0:16, :], kvw_v[...])[0:8]
    keyval = lookup(keyval, jnp.where((lane8 & 1) == 0, lane8 >> 1, 64 + (lane8 >> 1)))

    kv_src[...] = keyval
    kv_copies = []
    for k in range(1, NX):
        kv_copies.append(to_gx(k, kv_src, kv_dst.at[k], ks, kr))
        kv_copies[-1].start()
    started += kv_copies
    begin_projection(oa_v, ou_v)
    for copy in o_loads:
        copy.wait()
    down_rows = slice(16, 144)
    for c in range(FIRST):
        weight_chunk(oc_v, c, down_rows)

    for copy in z_copies:
        copy.wait_recv()
    summed = z_dst[0]
    for k in range(1, 4):
        summed = summed + z_dst[k]
    queries = []
    for m in range(4):
        magnitude = jnp.zeros((ROWS, 128), F32)
        for t in range(TENANTS):
            magnitude = jnp.where(
                tenant_of == t, qm_v[t : t + 1, 128 * m : 128 * m + 128], magnitude
            )
        queries.append(rope(summed[m] * (magnitude * lax.rsqrt(summed[4 + m]))))
    c1_src[0:16, :] = jnp.concatenate(queries[0:2], axis=0).astype(BF16)
    c1_src[16:32, :] = jnp.concatenate(queries[2:4], axis=0).astype(BF16)
    c1_dst[gy] = c1_src[...]
    c1_copies = []
    for k in range(1, NY):
        c1_copies.append(to_gy(k, c1_src, c1_dst.at[gy], c1s, c1r))
        c1_copies[-1].start()
    started += c1_copies
    for copy in kv_copies:
        copy.wait_recv()
    new = kv_src[...]
    for k in range(1, NX):
        new = new + kv_dst[k]
    new = jnp.where(gy < KV_HEADS, rope(new), new)
    new_src[...] = jnp.concatenate([new, jnp.zeros_like(new)], axis=0).astype(BF16)
    new_dst[gy] = new_src[...]
    new_copies = []
    for k in range(1, NY):
        new_copies.append(to_gy(k, new_src, new_dst.at[gy], news, newr))
        new_copies[-1].start()
    started += new_copies
    for c in range(FIRST, CHUNKS):
        weight_chunk(oc_v, c, down_rows)
    o_norms = joined(*norm_parts(o_gram))
    for i in range(8):
        flat_v[8 * i : 8 * i + 8, :] = o_norms[i]
    for r in range(ROWS):
        g_src[r, 1] = flat_v[pl.ds(r, 8, stride=8), :]

    page_no = lanes_of((ROWS, 96))
    row_no = rows_of((ROWS, 96))
    length = length_of[:, 0:96]
    live = page_no * PAGE < length
    remaining = jnp.clip(length - page_no * PAGE, 0, PAGE)
    table_pages = pt_v[...]

    def whole(x):
        return jnp.sum(jnp.sum(x.astype(F32), axis=1, keepdims=True), axis=0, keepdims=True)

    owner, filled = [], []
    for s in range(SLOTS):
        hit = jnp.logical_and(table_pages == (gx * NY + gy) * SLOTS + s, live)
        owner.append(whole(jnp.where(hit, row_no, 0)))
        filled.append(whole(jnp.where(hit, remaining, 0)))

    def same(a, b):
        return jnp.where(a == b, 1.0, 0.0).astype(F32)

    for copy in c1_copies:
        copy.wait_recv()
    c2_copy = to_partner(c1_dst, c2_dst, c2s, c2r)
    c2_copy.start()
    started.append(c2_copy)
    for j in range(NY):
        block = c1_dst[j].astype(F32)
        for m in range(4):
            qf_v[pl.ds(8 * j + 4 * core + m, 8, stride=HEADS), :] = block[8 * m : 8 * m + 8]
    c2_copy.wait_recv()
    for j in range(NY):
        block = c2_dst[j].astype(F32)
        for m in range(4):
            qf_v[pl.ds(8 * j + 4 - 4 * core + m, 8, stride=HEADS), :] = block[8 * m : 8 * m + 8]

    even_group = ((rows_of((HEADS, 128)) >> 4) & 1) == 0
    token = lanes_of((HEADS, PAGE)).astype(F32)
    peaks = []
    for s in range(SLOTS):
        q = jnp.zeros((HEADS, HEAD_DIM), F32)
        for r in range(ROWS):
            q = q + qf_v[r * HEADS : (r + 1) * HEADS, :] * same(owner[s], float(r))
        q = jnp.concatenate(
            [jnp.where(even_group, q, 0.0), jnp.where(even_group, 0.0, q)], axis=1
        ).astype(BF16)
        page_loads[s].wait()
        parts = [
            dot_nt(q[32 * p : 32 * p + 32], cache_v[s, 0, :, 256 * p : 256 * p + 256])
            for p in range(4)
        ]
        score = jnp.concatenate(parts, axis=0) * INV_ROOT
        score = jnp.where(token < filled[s], score, NEG_FILL)
        score_v[s] = score
        peaks.append(jnp.max(score, axis=1, keepdims=True))
    totals = []
    for s in range(SLOTS):
        peak = peaks[s]
        for other in range(SLOTS):
            if other != s:
                alike = owner[s] == owner[other]
                peak = jnp.maximum(peak, jnp.where(alike, peaks[other], NEG_FILL))
        weights = jnp.where(token < filled[s], jnp.exp(score_v[s] - peak), 0.0).astype(BF16)
        totals.append(jnp.sum(weights.astype(F32), axis=1, keepdims=True))
        for p in range(4):
            x = dot(weights[32 * p : 32 * p + 32], cache_v[s, 1, :, 256 * p : 256 * p + 256])
            num_v[s, 32 * p : 32 * p + 16, :] = x[0:16, 0:128]
            num_v[s, 32 * p + 16 : 32 * p + 32, :] = x[16:32, 128:256]
    lane_h = lanes_of((HEADS, 128))
    stats = jnp.zeros((HEADS, 128), F32)
    for r in range(ROWS):
        number = jnp.zeros((HEADS, HEAD_DIM), F32)
        peak = jnp.full((HEADS, 1), NEG_FILL, F32)
        total = jnp.zeros((HEADS, 1), F32)
        for s in range(SLOTS):
            mine = same(owner[s], float(r))
            number = number + num_v[s] * mine
            total = total + totals[s] * mine
            peak = jnp.maximum(peak, jnp.where(owner[s] == float(r), peaks[s], NEG_FILL))
        nbf_v[pl.ds(r, HEADS, stride=ROWS), :] = number
        stats = jnp.where(lane_h == r, peak, stats)
        stats = jnp.where(lane_h == 8 + r, total, stats)
    stats = three_parts(stats.T[0:16])
    stats = [x.astype(F32) for x in stats]
    lane16 = lanes_of((16, 128))
    for i in range(NX):
        n_src[i, 0:128, :] = nbf_v[128 * i : 128 * i + 128, :].astype(BF16)
        mine = [pltpu.roll(x, (16 * n - 16 * i) % 128, 1) if (n - i) % 8 else x for n, x in enumerate(stats)]
        n_src[i, 128:144, :] = jnp.where(
            lane16 < 16, mine[0], jnp.where(lane16 < 32, mine[1], mine[2])
        ).astype(BF16)

    n_copies = []
    for k in range(1, NX):
        peer = lax.rem(gx + k, NX)
        n_copies.append(to_gx(k, n_src.at[peer], n_dst.at[k], ns, nr))
        n_copies[-1].start()
    started += n_copies

    for copy in new_copies:
        copy.wait_recv()
    new_key = new_dst[gx].astype(F32)[0:8]
    new_value = new_dst[KV_HEADS + gx].astype(F32)[0:8]
    self_score = jnp.zeros((ROWS, 128), F32)
    for h in range(16):
        q = qf_v[pl.ds(16 * gx + h, 8, stride=HEADS), :]
        score = jnp.sum(q * new_key, axis=1, keepdims=True) * INV_ROOT
        self_score = jnp.where(lane8 == h, score, self_score)

    states = hid_v[:, pl.ds(pl.multiple_of(gy * 1024, 1024), 1024)].astype(F32)
    mine = tenant[gx]
    out_magnitude = jnp.zeros((8, 128), F32)
    for i in range(8):
        flat_v[8 * i : 8 * i + 8, :] = om_v[:, 128 * i : 128 * i + 128]
    for t in range(TENANTS):
        out_magnitude = jnp.where(mine == t, flat_v[pl.ds(t, 8, stride=8), :], out_magnitude)
    for i in range(8):
        flat_v[8 * i : 8 * i + 8, :] = states[:, 128 * i : 128 * i + 128]
    residual = flat_v[pl.ds(gx, 8, stride=8), :]

    def gathered(x, first):
        parts = [pltpu.roll(x, 128 - first - 16 * n, 1) if first + n else x for n in range(3)]
        return parts[0] + parts[1] + parts[2]

    for copy in n_copies:
        copy.wait_recv()
    n_dst[0] = n_src[gx]
    seen = [gathered(n_dst[k, 128:144, :].astype(F32), 0) for k in range(NX)]
    peak = seen[0][0:8]
    for k in range(1, NX):
        peak = jnp.maximum(peak, seen[k][0:8])
    total = jnp.zeros((ROWS, 128), F32)
    factors = []
    for k in range(NX):
        factors.append(jnp.exp(seen[k][0:8] - peak))
        total = total + factors[k] * seen[k][8:16]
    for j in range(8):
        pair = [jnp.zeros((ROWS, 128), F32), jnp.zeros((ROWS, 128), F32)]
        for k in range(NX):
            block = n_dst[k, 16 * j : 16 * j + 16, :].astype(F32)
            for n in range(2):
                h = 2 * j + n
                pair[n] = pair[n] + block[8 * n : 8 * n + 8] * factors[k][:, h : h + 1]
        e_src[16 * j : 16 * j + 16, :] = jnp.concatenate(pair, axis=0).astype(BF16)
    stats = jnp.zeros((ROWS, 128), F32)
    for n, x in enumerate(three_parts(peak) + three_parts(total)):
        x = x.astype(F32)
        x = pltpu.roll(x, 16 * n, 1) if n else x
        stats = jnp.where(jnp.logical_and(lane8 >= 16 * n, lane8 < 16 * n + 16), x, stats)
    e_src[128:144, :] = jnp.concatenate([stats, jnp.zeros_like(stats)], axis=0).astype(BF16)

    e_dst[gy] = e_src[...]
    e_copies = []
    for k in range(1, NY):
        e_copies.append(to_gy(k, e_src, e_dst.at[gy], es, er))
        e_copies[-1].start()
    started += e_copies
    for copy in e_copies:
        copy.wait_recv()
    peaks, totals = [], []
    peak = self_score
    for k in range(NY):
        x = e_dst[k, 128:144, :].astype(F32)[0:8]
        peaks.append(gathered(x, 0))
        totals.append(gathered(x, 48))
        peak = jnp.maximum(peak, peaks[k])
    own = jnp.exp(self_score - peak)
    total = own
    factors = []
    for k in range(NY):
        factors.append(jnp.exp(peaks[k] - peak))
        total = total + factors[k] * totals[k]
    for j in range(8):
        pair = [own[:, 2 * j + n : 2 * j + n + 1] * new_value for n in range(2)]
        for k in range(NY):
            block = e_dst[k, 16 * j : 16 * j + 16, :].astype(F32)
            for n in range(2):
                h = 2 * j + n
                pair[n] = pair[n] + block[8 * n : 8 * n + 8] * factors[k][:, h : h + 1]
        for n in range(2):
            h = 2 * j + n
            x = pair[n] / total[:, h : h + 1]
            att_v[:, 128 * h : 128 * h + 128] = jnp.concatenate([x, jnp.zeros_like(x)], axis=0).astype(BF16)

    attended = att_v[...]
    middle = dot_nt(attended, lhs_v[16:144, :])[0:8]
    extra = adapter(middle)
    projected = joined(
        dot(attended, we_v[...])[0:8] + extra[0], dot(attended, wo_v[...])[0:8] + extra[1]
    )
    for i in range(8):
        flat_v[8 * i : 8 * i + 8, :] = projected[i]
    for r in range(ROWS):
        g_src[r, 0] = flat_v[pl.ds(r, 8, stride=8), :]
    g_copies = []
    for k in range(1, NX):
        peer = lax.rem(gx + k, NX)
        g_copies.append(to_gx(k, g_src.at[peer], g_dst.at[k], gs, gr))
        g_copies[-1].start()
    started += g_copies

    summed = [g_src[gx, j] for j in range(2)]
    for copy in g_copies:
        copy.wait_recv()
    for k in range(1, NX):
        for j in range(2):
            summed[j] = summed[j] + g_dst[k, j]
    result = (residual + summed[0] * (out_magnitude * lax.rsqrt(summed[1])))
    for c in range(8):
        out[0:1, 128 * c : 128 * c + 128] = result[c : c + 1, :]
    for copy in started:
        copy.wait_send()


def local(
    hidden,
    norm_gain,
    q_codes,
    q_absmax,
    kv_codes,
    kv_absmax,
    o_codes,
    o_absmax,
    q_down,
    q_up,
    q_magnitude,
    o_down,
    o_up,
    o_magnitude,
    tenant,
    lengths,
    page_table,
    kv_cache,
):
    def down_rows(down):
        return jnp.transpose(down, (0, 2, 1)).reshape(TENANTS * RANK, LOCAL_IN)

    def up_rows(up):
        return up.reshape(TENANTS * RANK, 1024)

    vmem = pltpu.VMEM
    dma = pltpu.SemaphoreType.DMA
    hbm = pl.BlockSpec(memory_space=pl.ANY)
    scratch = [
        pltpu.SMEM((8,), jnp.int32),
        pltpu.SMEM((8,), jnp.int32),
        vmem((8, D), BF16),
        vmem((16, 128), F32),
        vmem((LOCAL_IN, HALF), jnp.int32),
        vmem((32, 1024), F32),
        vmem((64, LOCAL_IN), jnp.int32),
        vmem((32, 128), F32),
        vmem((LOCAL_IN, HALF), jnp.int32),
        vmem((32, 1024), F32),
        vmem((128, LOCAL_IN), BF16),
        vmem((128, 1024), BF16),
        vmem((8, HALF), F32),
        vmem((128, LOCAL_IN), BF16),
        vmem((128, 1024), BF16),
        vmem((8, 1024), F32),
        vmem((8, 96), jnp.int32),
        vmem((SLOTS, 2, PAGE, 1024), BF16),
        vmem((24, 128), F32),
        vmem((4, 32, 128), F32),
        vmem((4, 32, 128), F32),
        vmem((2, 128, HALF), BF16),
        vmem((144, LOCAL_IN), BF16),
        vmem((LOCAL_IN, HALF), BF16),
        vmem((LOCAL_IN, HALF), BF16),
        vmem((2, 144, HALF), F32),
        vmem((2, 8, HALF), F32),
        vmem((64, 128), F32),
        vmem((128, LOCAL_IN), BF16),
        vmem((ROWS * HEADS, HEAD_DIM), F32),
        vmem((SLOTS, HEADS, PAGE), F32),
        vmem((SLOTS, HEADS, HEAD_DIM), F32),
        vmem((ROWS * HEADS, HEAD_DIM), F32),
        vmem((16, LOCAL_IN), BF16),
        vmem((2, 8, 8, 128), F32),
        vmem((8, 8, 128), F32),
        vmem((8, 8, 128), F32),
        vmem((4, 8, 8, 128), F32),
        vmem((32, 128), BF16),
        vmem((NY, 32, 128), BF16),
        vmem((NY, 32, 128), BF16),
        vmem((8, 128), F32),
        vmem((NX, 8, 128), F32),
        vmem((16, 128), BF16),
        vmem((NY, 16, 128), BF16),
        vmem((NX, 144, 128), BF16),
        vmem((NX, 144, 128), BF16),
        vmem((144, 128), BF16),
        vmem((NY, 144, 128), BF16),
        vmem((NX, 2, 8, 128), F32),
        vmem((NX, 2, 8, 128), F32),
        dma((16,)),
        dma((CHUNKS + 1,)),
        dma((SLOTS,)),
        dma((1,)),
        dma((1,)),
        dma((NX,)),
        dma((NX,)),
        dma((NY,)),
        dma((NY,)),
        dma((1,)),
        dma((1,)),
        dma((NX,)),
        dma((NX,)),
        dma((NY,)),
        dma((NY,)),
        dma((NX,)),
        dma((NX,)),
        dma((NY,)),
        dma((NY,)),
        dma((NX,)),
        dma((NX,)),
    ]
    result = pl.pallas_call(
        kernel,
        out_shape=jax.ShapeDtypeStruct((1, 1024), F32),
        in_specs=[hbm] * 19,
        out_specs=pl.BlockSpec(memory_space=pltpu.VMEM),
        scratch_shapes=scratch,
        compiler_params=pltpu.CompilerParams(
            collective_id=0, has_side_effects=True, vmem_limit_bytes=56 * 1024 * 1024
        ),
        name="layer",
    )(
        tenant,
        lengths,
        hidden,
        norm_gain.reshape(128, 128),
        q_codes,
        q_absmax,
        kv_codes.T,
        kv_absmax,
        o_codes,
        o_absmax,
        down_rows(q_down),
        up_rows(q_up),
        q_magnitude,
        down_rows(o_down),
        up_rows(o_up),
        o_magnitude,
        page_table,
        kv_cache,
        jnp.asarray(constants()),
    )
    return result.astype(BF16)


def solution(mesh):
    in_specs = (
        P(),
        P(),
        P("gx", "gy"),
        P("gx", "gy"),
        P("gx", "gy"),
        P("gx", "gy"),
        P("gx", "gy"),
        P("gx", "gy"),
        P(None, "gx", None),
        P(None, None, "gy"),
        P(None, "gy"),
        P(None, "gx", None),
        P(None, None, "gy"),
        P(None, "gy"),
        P(),
        P(),
        P(),
        P(("gx", "gy"), None, None, None),
    )
    return jax.shard_map(
        local, mesh=mesh, in_specs=in_specs, out_specs=P("gx", "gy"), check_vma=False
    )
```

```python
import functools
import math

import jax
import jax.numpy as jnp
import numpy as np
from jax import lax
from jax.experimental import pallas as pl
from jax.experimental.pallas import tpu as pltpu
from jax.sharding import PartitionSpec as P

HEADS = 128
KV_HEADS = 8
HEAD_DIM = 128
TENANTS = 8
RANK = 16
QBLOCK = 64
PAGE = 256
ROWS = 8
NX = 8
NY = 16
SLOTS = 5
LOCAL_IN = 2048
HALF = 512
CHUNK = 512
CHUNKS = LOCAL_IN // CHUNK
LATER = 2
FIRST = 1
D = 16384

NF4_LEVELS = (
    -1.0,
    -0.6961928009986877,
    -0.5250730514526367,
    -0.39491748809814453,
    -0.28444138169288635,
    -0.18477343022823334,
    -0.09105003625154495,
    0.0,
    0.07958029955625534,
    0.16093020141124725,
    0.24611230194568634,
    0.33791524171829224,
    0.44070982933044434,
    0.5626170039176941,
    0.7229568362236023,
    1.0,
)
NORM_EPS = 1e-05
NEG_FILL = -1e30
ROPE_BASE = 500000.0
MESH = pl.DeviceIdType.MESH
F32 = jnp.float32
BF16 = jnp.bfloat16
INV_ROOT = 1.0 / math.sqrt(HEAD_DIM)


def constants():
    table = np.zeros((24, 128), np.float32)
    table[:16] = np.asarray(NF4_LEVELS, np.float32)[:, None]
    frequency = ROPE_BASE ** (-2.0 * np.arange(64, dtype=np.float64) / HEAD_DIM)
    table[16:] = np.concatenate([frequency, frequency]).astype(np.float32)[None]
    return table


def lookup(table, index):
    numbers = lax.GatherDimensionNumbers(
        offset_dims=(),
        collapsed_slice_dims=(1,),
        start_index_map=(1,),
        operand_batching_dims=(0,),
        start_indices_batching_dims=(0,),
    )
    return lax.gather(
        table,
        index[..., None],
        numbers,
        slice_sizes=(1, 1),
        mode=lax.GatherScatterMode.PROMISE_IN_BOUNDS,
    )


def levels(tables, words, high):
    numbers = lax.GatherDimensionNumbers(
        offset_dims=(),
        collapsed_slice_dims=(0,),
        start_index_map=(0,),
        operand_batching_dims=(1,),
        start_indices_batching_dims=(1,),
    )

    def pick(table, index):
        return lax.gather(
            table,
            index[..., None],
            numbers,
            slice_sizes=(1, 1),
            mode=lax.GatherScatterMode.PROMISE_IN_BOUNDS,
        )

    parts = []
    for j in range(words.shape[0] // 8):
        part = words[8 * j : 8 * j + 8]
        at = (part >> 4 if high else part) & 7
        upper = part > 127 if high else (part & 8) != 0
        parts.append(jnp.where(upper, pick(tables[1], at), pick(tables[0], at)))
    return jnp.concatenate(parts, axis=0)


def lanes_of(shape):
    return lax.broadcasted_iota(jnp.int32, shape, 1)


def rows_of(shape):
    return lax.broadcasted_iota(jnp.int32, shape, 0)


def dot(a, b):
    return lax.dot_general(a, b, (((1,), (0,)), ((), ())), preferred_element_type=F32)


def dot_nt(a, b):
    return lax.dot_general(a, b, (((1,), (1,)), ((), ())), preferred_element_type=F32)


def two_parts(x):
    high = x.astype(BF16)
    return high, (x - high.astype(F32)).astype(BF16)


def three_parts(x):
    high = x.astype(BF16)
    rest = x - high.astype(F32)
    middle = rest.astype(BF16)
    return [high, middle, (rest - middle.astype(F32)).astype(BF16)]


def even_first():
    row, lane = rows_of((256, 256)), lanes_of((256, 256))
    return jnp.where(row == jnp.where(lane < 128, 2 * lane, 2 * lane - 255), 1.0, 0.0).astype(BF16)


def joined(even, odd):
    n, width = even.shape
    lane = lanes_of((n, 128))
    is_even = (lane & 1) == 0
    blocks = []
    for c in range(width // 64):
        part = slice(128 * (c // 2), 128 * (c // 2) + 128)
        at = 64 * (c % 2) + (lane >> 1)
        blocks.append(jnp.where(is_even, lookup(even[:, part], at), lookup(odd[:, part], at)))
    return blocks


def kernel(
    tenant_h,
    lengths_h,
    hidden,
    gain,
    q_codes,
    q_absmax,
    kv_codes,
    kv_absmax,
    o_codes,
    o_absmax,
    q_down,
    q_up,
    q_magnitude,
    o_down,
    o_up,
    o_magnitude,
    pages,
    cache,
    consts,
    out,
    tenant,
    lengths,
    hid_v,
    gain_v,
    qc_v,
    qa_v,
    kc_v,
    ka_v,
    oc_v,
    oa_v,
    qd_v,
    qu_v,
    qm_v,
    od_v,
    ou_v,
    om_v,
    pt_v,
    cache_v,
    const_v,
    ae_v,
    ao_v,
    up_v,
    lhs_v,
    we_v,
    wo_v,
    acc_v,
    sq_v,
    flat_v,
    kvw_v,
    qf_v,
    score_v,
    num_v,
    nbf_v,
    att_v,
    b_src,
    b_dst,
    z_src,
    z_dst,
    c1_src,
    c1_dst,
    c2_dst,
    kv_src,
    kv_dst,
    new_src,
    new_dst,
    n_src,
    n_dst,
    e_src,
    e_dst,
    g_src,
    g_dst,
    load_sem,
    code_sem,
    page_sem,
    bs,
    br,
    zs,
    zr,
    c1s,
    c1r,
    c2s,
    c2r,
    ks,
    kr,
    news,
    newr,
    ns,
    nr,
    es,
    er,
    gs,
    gr,
):
    gx = lax.axis_index("gx")
    gy = lax.axis_index("gy")

    def load(n, src, dst):
        copy = pltpu.make_async_copy(src, dst, load_sem.at[n])
        copy.start()
        return copy

    in_at = pl.multiple_of(gx * LOCAL_IN, LOCAL_IN)
    core = lax.rem(gx, 2)
    partner = gx + 1 - 2 * core
    z = lax.div(gx, 2)
    heads_at = pl.multiple_of(core * HALF, HALF)
    loads = [
        load(14, tenant_h, tenant),
        load(15, lengths_h, lengths),
        load(0, hidden, hid_v),
        load(1, gain.at[pl.ds(pl.multiple_of(gx * 16, 16), 16), :], gain_v),
        load(2, consts, const_v),
        load(4, q_down, qd_v),
        load(3, q_absmax, qa_v),
        load(5, q_up, qu_v),
    ]
    q_loads = []
    for c in range(CHUNKS):
        part = pl.ds(c * CHUNK, CHUNK)
        q_loads.append(pltpu.make_async_copy(q_codes.at[part, :], qc_v.at[part, :], code_sem.at[c]))
        q_loads[-1].start()
    barrier = pltpu.get_barrier_semaphore()
    for k in range(1, NX):
        pl.semaphore_signal(
            barrier, inc=1, device_id={"gx": lax.rem(gx + k, NX)}, device_id_type=MESH
        )
    for k in range(1, NY):
        pl.semaphore_signal(
            barrier, inc=1, device_id={"gy": lax.rem(gy + k, NY)}, device_id_type=MESH
        )

    def to_partner(src, dst, send, recv):
        return pltpu.make_async_remote_copy(
            src_ref=src,
            dst_ref=dst,
            send_sem=send.at[0],
            recv_sem=recv.at[0],
            device_id={"gx": partner},
            device_id_type=MESH,
        )

    def to_gx(k, src, dst, send, recv):
        return pltpu.make_async_remote_copy(
            src_ref=src,
            dst_ref=dst,
            send_sem=send.at[k],
            recv_sem=recv.at[k],
            device_id={"gx": lax.rem(gx + k, NX)},
            device_id_type=MESH,
        )

    def to_gy(k, src, dst, send, recv):
        return pltpu.make_async_remote_copy(
            src_ref=src,
            dst_ref=dst,
            send_sem=send.at[k],
            recv_sem=recv.at[k],
            device_id={"gy": lax.rem(gy + k, NY)},
            device_id_type=MESH,
        )

    started = []

    for copy in loads[0:5]:
        copy.wait()

    row8 = rows_of((ROWS, 128))
    lane8 = lanes_of((ROWS, 128))
    tenant_of = jnp.zeros((ROWS, 128), jnp.int32)
    length_of = jnp.zeros((ROWS, 128), jnp.int32)
    for r in range(ROWS):
        tenant_of = jnp.where(row8 == r, tenant[r], tenant_of)
        length_of = jnp.where(row8 == r, lengths[r], length_of)
    angles = length_of.astype(F32) * const_v[16:24, :]
    cosine = jnp.cos(angles)
    sine = jnp.sin(angles)
    sine = jnp.where(lane8 < 64, -sine, sine)

    def rope(x):
        return x * cosine + pltpu.roll(x, 64, 1) * sine

    total = jnp.zeros((ROWS, 128), F32)
    for c in range(D // 1024):
        x = hid_v[:, c * 1024 : (c + 1) * 1024].astype(F32)
        x = x * x
        for j in range(8):
            total = total + x[:, j * 128 : (j + 1) * 128]
    inverse = lax.rsqrt(jnp.sum(total, axis=1, keepdims=True) * (1.0 / D) + NORM_EPS)
    states = hid_v[:, pl.ds(in_at, LOCAL_IN)].astype(F32)
    lhs_v[0:16, :] = jnp.zeros((16, LOCAL_IN), BF16)
    normed = []
    for c in range(16):
        x = states[:, c * 128 : (c + 1) * 128] * inverse * gain_v[c : c + 1, :]
        normed.append(x)
    normed = jnp.concatenate(normed, axis=1)
    lhs_v[0:16, :] = jnp.concatenate([normed, jnp.zeros_like(normed)], axis=0).astype(BF16)
    for copy in loads[5:]:
        copy.wait()
    lhs_v[16:144, :] = qd_v[...]

    lane64 = lanes_of((64, 128))
    tables = (const_v[0:8, :], const_v[8:16, :])
    parting = even_first()

    def dequantize(codes, row, scale_row):
        for c in range(4):
            cols = slice(128 * c, 128 * c + 128)
            words = codes[pl.ds(row, 64), cols]
            for half, (scales, ref) in enumerate(((ae_v, we_v), (ao_v, wo_v))):
                value = levels(tables, words, half == 1) * scales[c, pl.ds(scale_row, 1), :]
                ref[pl.ds(row, 64), cols] = value.astype(BF16)
                square = value * value
                part = square[0:8]
                for j in range(1, 8):
                    part = part + square[8 * j : 8 * j + 8]
                sq_v[half, :, cols] += part

    def weight_chunk(codes, c, lhs_rows):
        base = c * CHUNK
        for b in range(CHUNK // QBLOCK):
            dequantize(codes, base + b * QBLOCK, c * (CHUNK // QBLOCK) + b)
        left = lhs_v[lhs_rows, pl.ds(base, CHUNK)]
        acc_v[0, lhs_rows, :] += dot(left, we_v[pl.ds(base, CHUNK), :])
        acc_v[1, lhs_rows, :] += dot(left, wo_v[pl.ds(base, CHUNK), :])

    def begin_projection(absmax, up):
        for c in range(4):
            part = slice(256 * c, 256 * c + 256)
            parts = dot(jnp.concatenate(three_parts(absmax[:, part]), axis=0), parting)
            whole = parts[0:32] + parts[32:64] + parts[64:96]
            ae_v[c] = whole[:, 0:128]
            ao_v[c] = whole[:, 128:256]
            both = dot(up[:, part], parting).astype(BF16)
            up_v[0, :, 128 * c : 128 * c + 128] = both[:, 0:128]
            up_v[1, :, 128 * c : 128 * c + 128] = both[:, 128:256]
        acc_v[...] = jnp.zeros_like(acc_v)
        sq_v[...] = jnp.zeros_like(sq_v)

    def norm_parts(gram):
        same = (rows_of((128, 128)) >> 4) == (lanes_of((128, 128)) >> 4)
        high, low = two_parts(jnp.where(same, gram, 0.0))
        halves = []
        for half in range(2):
            up = up_v[half]
            inner = 2.0 * acc_v[half, 16:144, :] + (dot(high, up) + dot(low, up))
            terms = jnp.sum((up.astype(F32) * inner).reshape(TENANTS, RANK, HALF), axis=1)
            terms = terms + jnp.sum(sq_v[half], axis=0, keepdims=True)
            mine = tenant_of[:, 0:1]
            chosen = jnp.zeros((ROWS, HALF), F32)
            for t in range(TENANTS):
                chosen = jnp.where(mine == t, terms[t : t + 1, :], chosen)
            halves.append(chosen)
        return halves

    def adapter(middle):
        masked = jnp.where(tenant_of == (lane8 >> 4), middle, 0.0)
        high = masked.astype(BF16).astype(F32)
        both = jnp.concatenate([high, masked - high], axis=0).astype(BF16)
        halves = []
        for half in range(2):
            x = dot(both, up_v[half])
            halves.append(x[0:8] + x[8:16])
        return halves


    begin_projection(qa_v, qu_v)

    inner = dot_nt(lhs_v[...], lhs_v[16:144, :])
    middle, gram = inner[0:8], inner[16:144]

    for c in range(CHUNKS):
        q_loads[c].wait()
        if c == LATER:
            later = [
                load(6, kv_codes, kc_v),
                load(7, kv_absmax, ka_v),
                load(8, q_magnitude.at[:, pl.ds(heads_at, HALF)], qm_v),
                load(9, pages, pt_v),
            ]
            o_small = [load(10, o_absmax, oa_v), load(11, o_down, od_v), load(12, o_up, ou_v), load(13, o_magnitude, om_v)]
            o_loads = [pltpu.make_async_copy(o_codes, oc_v, code_sem.at[CHUNKS])]
            o_loads[0].start()
            page_loads = []
            for s in range(SLOTS):
                page_loads.append(pltpu.make_async_copy(cache.at[s], cache_v.at[s], page_sem.at[s]))
                page_loads[-1].start()

        weight_chunk(qc_v, c, slice(0, 144))

    extra = adapter(middle)
    product = joined(acc_v[0, 0:8, :] + extra[0], acc_v[1, 0:8, :] + extra[1])
    norms = joined(*norm_parts(gram))
    for half in range(2):
        for m in range(4):
            b_src[half, m] = product[4 * half + m]
            b_src[half, 4 + m] = norms[4 * half + m]

    pl.semaphore_wait(barrier, NX - 1 + NY - 1)

    b_copy = to_partner(b_src.at[1 - core], b_dst, bs, br)
    b_copy.start()
    started.append(b_copy)
    for copy in o_small:
        copy.wait()
    lhs_v[16:144, :] = od_v[...]
    o_gram = dot_nt(lhs_v[16:144, :], lhs_v[16:144, :])
    b_copy.wait_recv()
    z_src[...] = b_src[core] + b_dst[...]
    z_dst[z] = z_src[...]
    z_copies = []
    for k in range(1, 4):
        z_copies.append(to_gx(2 * k, z_src, z_dst.at[z], zs, zr))
        z_copies[-1].start()
    started += z_copies

    for copy in later:
        copy.wait()
    lane32 = lanes_of((32, 128))
    at = jnp.where(lane32 < 64, 2 * lane32, 2 * lane32 - 127)
    kv_scale = jnp.concatenate(
        [lookup(ka_v[...], at), jnp.zeros((96, 128), F32)], axis=0
    ).T
    for c in range(16):
        words = kc_v[:, c * 128 : (c + 1) * 128]
        for half in range(2):
            scale = lookup(kv_scale[64 * half : 64 * half + 64], 2 * c + (lane64 >> 6))
            kvw_v[64 * half : 64 * half + 64, c * 128 : (c + 1) * 128] = (
                levels(tables, words, half == 1) * scale
            ).astype(BF16)
    keyval = dot_nt(lhs_v[0:16, :], kvw_v[...])[0:8]
    keyval = lookup(keyval, jnp.where((lane8 & 1) == 0, lane8 >> 1, 64 + (lane8 >> 1)))

    kv_src[...] = keyval
    kv_copies = []
    for k in range(1, NX):
        kv_copies.append(to_gx(k, kv_src, kv_dst.at[k], ks, kr))
        kv_copies[-1].start()
    started += kv_copies
    begin_projection(oa_v, ou_v)
    for copy in o_loads:
        copy.wait()
    down_rows = slice(16, 144)
    for c in range(FIRST):
        weight_chunk(oc_v, c, down_rows)

    for copy in z_copies:
        copy.wait_recv()
    summed = z_dst[0]
    for k in range(1, 4):
        summed = summed + z_dst[k]
    queries = []
    for m in range(4):
        magnitude = jnp.zeros((ROWS, 128), F32)
        for t in range(TENANTS):
            magnitude = jnp.where(
                tenant_of == t, qm_v[t : t + 1, 128 * m : 128 * m + 128], magnitude
            )
        queries.append(rope(summed[m] * (magnitude * lax.rsqrt(summed[4 + m]))))
    c1_src[0:16, :] = jnp.concatenate(queries[0:2], axis=0).astype(BF16)
    c1_src[16:32, :] = jnp.concatenate(queries[2:4], axis=0).astype(BF16)
    c1_dst[gy] = c1_src[...]
    c1_copies = []
    for k in range(1, NY):
        c1_copies.append(to_gy(k, c1_src, c1_dst.at[gy], c1s, c1r))
        c1_copies[-1].start()
    started += c1_copies
    for copy in kv_copies:
        copy.wait_recv()
    new = kv_src[...]
    for k in range(1, NX):
        new = new + kv_dst[k]
    new = jnp.where(gy < KV_HEADS, rope(new), new)
    new_src[...] = jnp.concatenate([new, jnp.zeros_like(new)], axis=0).astype(BF16)
    new_dst[gy] = new_src[...]
    new_copies = []
    for k in range(1, NY):
        new_copies.append(to_gy(k, new_src, new_dst.at[gy], news, newr))
        new_copies[-1].start()
    started += new_copies
    for c in range(FIRST, CHUNKS):
        weight_chunk(oc_v, c, down_rows)
    o_norms = joined(*norm_parts(o_gram))
    for i in range(8):
        flat_v[8 * i : 8 * i + 8, :] = o_norms[i]
    for r in range(ROWS):
        g_src[r, 1] = flat_v[pl.ds(r, 8, stride=8), :]

    page_no = lanes_of((ROWS, 96))
    row_no = rows_of((ROWS, 96))
    length = length_of[:, 0:96]
    live = page_no * PAGE < length
    remaining = jnp.clip(length - page_no * PAGE, 0, PAGE)
    table_pages = pt_v[...]

    def whole(x):
        return jnp.sum(jnp.sum(x.astype(F32), axis=1, keepdims=True), axis=0, keepdims=True)

    owner, filled = [], []
    for s in range(SLOTS):
        hit = jnp.logical_and(table_pages == (gx * NY + gy) * SLOTS + s, live)
        owner.append(whole(jnp.where(hit, row_no, 0)))
        filled.append(whole(jnp.where(hit, remaining, 0)))

    def same(a, b):
        return jnp.where(a == b, 1.0, 0.0).astype(F32)

    for copy in c1_copies:
        copy.wait_recv()
    c2_copy = to_partner(c1_dst, c2_dst, c2s, c2r)
    c2_copy.start()
    started.append(c2_copy)
    for j in range(NY):
        block = c1_dst[j].astype(F32)
        for m in range(4):
            qf_v[pl.ds(8 * j + 4 * core + m, 8, stride=HEADS), :] = block[8 * m : 8 * m + 8]
    c2_copy.wait_recv()
    for j in range(NY):
        block = c2_dst[j].astype(F32)
        for m in range(4):
            qf_v[pl.ds(8 * j + 4 - 4 * core + m, 8, stride=HEADS), :] = block[8 * m : 8 * m + 8]

    even_group = ((rows_of((HEADS, 128)) >> 4) & 1) == 0
    token = lanes_of((HEADS, PAGE)).astype(F32)
    peaks = []
    for s in range(SLOTS):
        q = jnp.zeros((HEADS, HEAD_DIM), F32)
        for r in range(ROWS):
            q = q + qf_v[r * HEADS : (r + 1) * HEADS, :] * same(owner[s], float(r))
        q = jnp.concatenate(
            [jnp.where(even_group, q, 0.0), jnp.where(even_group, 0.0, q)], axis=1
        ).astype(BF16)
        page_loads[s].wait()
        parts = [
            dot_nt(q[32 * p : 32 * p + 32], cache_v[s, 0, :, 256 * p : 256 * p + 256])
            for p in range(4)
        ]
        score = jnp.concatenate(parts, axis=0) * INV_ROOT
        score = jnp.where(token < filled[s], score, NEG_FILL)
        score_v[s] = score
        peaks.append(jnp.max(score, axis=1, keepdims=True))
    totals = []
    for s in range(SLOTS):
        peak = peaks[s]
        for other in range(SLOTS):
            if other != s:
                alike = owner[s] == owner[other]
                peak = jnp.maximum(peak, jnp.where(alike, peaks[other], NEG_FILL))
        weights = jnp.where(token < filled[s], jnp.exp(score_v[s] - peak), 0.0).astype(BF16)
        totals.append(jnp.sum(weights.astype(F32), axis=1, keepdims=True))
        for p in range(4):
            x = dot(weights[32 * p : 32 * p + 32], cache_v[s, 1, :, 256 * p : 256 * p + 256])
            num_v[s, 32 * p : 32 * p + 16, :] = x[0:16, 0:128]
            num_v[s, 32 * p + 16 : 32 * p + 32, :] = x[16:32, 128:256]
    lane_h = lanes_of((HEADS, 128))
    stats = jnp.zeros((HEADS, 128), F32)
    for r in range(ROWS):
        number = jnp.zeros((HEADS, HEAD_DIM), F32)
        peak = jnp.full((HEADS, 1), NEG_FILL, F32)
        total = jnp.zeros((HEADS, 1), F32)
        for s in range(SLOTS):
            mine = same(owner[s], float(r))
            number = number + num_v[s] * mine
            total = total + totals[s] * mine
            peak = jnp.maximum(peak, jnp.where(owner[s] == float(r), peaks[s], NEG_FILL))
        nbf_v[pl.ds(r, HEADS, stride=ROWS), :] = number
        stats = jnp.where(lane_h == r, peak, stats)
        stats = jnp.where(lane_h == 8 + r, total, stats)
    stats = three_parts(stats.T[0:16])
    stats = [x.astype(F32) for x in stats]
    lane16 = lanes_of((16, 128))
    for i in range(NX):
        n_src[i, 0:128, :] = nbf_v[128 * i : 128 * i + 128, :].astype(BF16)
        mine = [pltpu.roll(x, (16 * n - 16 * i) % 128, 1) if (n - i) % 8 else x for n, x in enumerate(stats)]
        n_src[i, 128:144, :] = jnp.where(
            lane16 < 16, mine[0], jnp.where(lane16 < 32, mine[1], mine[2])
        ).astype(BF16)

    n_copies = []
    for k in range(1, NX):
        peer = lax.rem(gx + k, NX)
        n_copies.append(to_gx(k, n_src.at[peer], n_dst.at[k], ns, nr))
        n_copies[-1].start()
    started += n_copies

    for copy in new_copies:
        copy.wait_recv()
    new_key = new_dst[gx].astype(F32)[0:8]
    new_value = new_dst[KV_HEADS + gx].astype(F32)[0:8]
    self_score = jnp.zeros((ROWS, 128), F32)
    for h in range(16):
        q = qf_v[pl.ds(16 * gx + h, 8, stride=HEADS), :]
        score = jnp.sum(q * new_key, axis=1, keepdims=True) * INV_ROOT
        self_score = jnp.where(lane8 == h, score, self_score)

    states = hid_v[:, pl.ds(pl.multiple_of(gy * 1024, 1024), 1024)].astype(F32)
    mine = tenant[gx]
    out_magnitude = jnp.zeros((8, 128), F32)
    for i in range(8):
        flat_v[8 * i : 8 * i + 8, :] = om_v[:, 128 * i : 128 * i + 128]
    for t in range(TENANTS):
        out_magnitude = jnp.where(mine == t, flat_v[pl.ds(t, 8, stride=8), :], out_magnitude)
    for i in range(8):
        flat_v[8 * i : 8 * i + 8, :] = states[:, 128 * i : 128 * i + 128]
    residual = flat_v[pl.ds(gx, 8, stride=8), :]

    def gathered(x, first):
        parts = [pltpu.roll(x, 128 - first - 16 * n, 1) if first + n else x for n in range(3)]
        return parts[0] + parts[1] + parts[2]

    for copy in n_copies:
        copy.wait_recv()
    n_dst[0] = n_src[gx]
    seen = [gathered(n_dst[k, 128:144, :].astype(F32), 0) for k in range(NX)]
    peak = seen[0][0:8]
    for k in range(1, NX):
        peak = jnp.maximum(peak, seen[k][0:8])
    total = jnp.zeros((ROWS, 128), F32)
    factors = []
    for k in range(NX):
        factors.append(jnp.exp(seen[k][0:8] - peak))
        total = total + factors[k] * seen[k][8:16]
    for j in range(8):
        pair = [jnp.zeros((ROWS, 128), F32), jnp.zeros((ROWS, 128), F32)]
        for k in range(NX):
            block = n_dst[k, 16 * j : 16 * j + 16, :].astype(F32)
            for n in range(2):
                h = 2 * j + n
                pair[n] = pair[n] + block[8 * n : 8 * n + 8] * factors[k][:, h : h + 1]
        e_src[16 * j : 16 * j + 16, :] = jnp.concatenate(pair, axis=0).astype(BF16)
    stats = jnp.zeros((ROWS, 128), F32)
    for n, x in enumerate(three_parts(peak) + three_parts(total)):
        x = x.astype(F32)
        x = pltpu.roll(x, 16 * n, 1) if n else x
        stats = jnp.where(jnp.logical_and(lane8 >= 16 * n, lane8 < 16 * n + 16), x, stats)
    e_src[128:144, :] = jnp.concatenate([stats, jnp.zeros_like(stats)], axis=0).astype(BF16)

    e_dst[gy] = e_src[...]
    e_copies = []
    for k in range(1, NY):
        e_copies.append(to_gy(k, e_src, e_dst.at[gy], es, er))
        e_copies[-1].start()
    started += e_copies
    for copy in e_copies:
        copy.wait_recv()
    peaks, totals = [], []
    peak = self_score
    for k in range(NY):
        x = e_dst[k, 128:144, :].astype(F32)[0:8]
        peaks.append(gathered(x, 0))
        totals.append(gathered(x, 48))
        peak = jnp.maximum(peak, peaks[k])
    own = jnp.exp(self_score - peak)
    total = own
    factors = []
    for k in range(NY):
        factors.append(jnp.exp(peaks[k] - peak))
        total = total + factors[k] * totals[k]
    for j in range(8):
        pair = [own[:, 2 * j + n : 2 * j + n + 1] * new_value for n in range(2)]
        for k in range(NY):
            block = e_dst[k, 16 * j : 16 * j + 16, :].astype(F32)
            for n in range(2):
                h = 2 * j + n
                pair[n] = pair[n] + block[8 * n : 8 * n + 8] * factors[k][:, h : h + 1]
        for n in range(2):
            h = 2 * j + n
            x = pair[n] / total[:, h : h + 1]
            att_v[:, 128 * h : 128 * h + 128] = jnp.concatenate([x, jnp.zeros_like(x)], axis=0).astype(BF16)

    attended = att_v[...]
    middle = dot_nt(attended, lhs_v[16:144, :])[0:8]
    extra = adapter(middle)
    projected = joined(
        dot(attended, we_v[...])[0:8] + extra[0], dot(attended, wo_v[...])[0:8] + extra[1]
    )
    for i in range(8):
        flat_v[8 * i : 8 * i + 8, :] = projected[i]
    for r in range(ROWS):
        g_src[r, 0] = flat_v[pl.ds(r, 8, stride=8), :]
    g_copies = []
    for k in range(1, NX):
        peer = lax.rem(gx + k, NX)
        g_copies.append(to_gx(k, g_src.at[peer], g_dst.at[k], gs, gr))
        g_copies[-1].start()
    started += g_copies

    summed = [g_src[gx, j] for j in range(2)]
    for copy in g_copies:
        copy.wait_recv()
    for k in range(1, NX):
        for j in range(2):
            summed[j] = summed[j] + g_dst[k, j]
    result = (residual + summed[0] * (out_magnitude * lax.rsqrt(summed[1])))
    for c in range(8):
        out[0:1, 128 * c : 128 * c + 128] = result[c : c + 1, :]
    for copy in started:
        copy.wait_send()


def local(
    hidden,
    norm_gain,
    q_codes,
    q_absmax,
    kv_codes,
    kv_absmax,
    o_codes,
    o_absmax,
    q_down,
    q_up,
    q_magnitude,
    o_down,
    o_up,
    o_magnitude,
    tenant,
    lengths,
    page_table,
    kv_cache,
):
    def down_rows(down):
        return jnp.transpose(down, (0, 2, 1)).reshape(TENANTS * RANK, LOCAL_IN)

    def up_rows(up):
        return up.reshape(TENANTS * RANK, 1024)

    vmem = pltpu.VMEM
    dma = pltpu.SemaphoreType.DMA
    hbm = pl.BlockSpec(memory_space=pl.ANY)
    scratch = [
        pltpu.SMEM((8,), jnp.int32),
        pltpu.SMEM((8,), jnp.int32),
        vmem((8, D), BF16),
        vmem((16, 128), F32),
        vmem((LOCAL_IN, HALF), jnp.int32),
        vmem((32, 1024), F32),
        vmem((64, LOCAL_IN), jnp.int32),
        vmem((32, 128), F32),
        vmem((LOCAL_IN, HALF), jnp.int32),
        vmem((32, 1024), F32),
        vmem((128, LOCAL_IN), BF16),
        vmem((128, 1024), BF16),
        vmem((8, HALF), F32),
        vmem((128, LOCAL_IN), BF16),
        vmem((128, 1024), BF16),
        vmem((8, 1024), F32),
        vmem((8, 96), jnp.int32),
        vmem((SLOTS, 2, PAGE, 1024), BF16),
        vmem((24, 128), F32),
        vmem((4, 32, 128), F32),
        vmem((4, 32, 128), F32),
        vmem((2, 128, HALF), BF16),
        vmem((144, LOCAL_IN), BF16),
        vmem((LOCAL_IN, HALF), BF16),
        vmem((LOCAL_IN, HALF), BF16),
        vmem((2, 144, HALF), F32),
        vmem((2, 8, HALF), F32),
        vmem((64, 128), F32),
        vmem((128, LOCAL_IN), BF16),
        vmem((ROWS * HEADS, HEAD_DIM), F32),
        vmem((SLOTS, HEADS, PAGE), F32),
        vmem((SLOTS, HEADS, HEAD_DIM), F32),
        vmem((ROWS * HEADS, HEAD_DIM), F32),
        vmem((16, LOCAL_IN), BF16),
        vmem((2, 8, 8, 128), F32),
        vmem((8, 8, 128), F32),
        vmem((8, 8, 128), F32),
        vmem((4, 8, 8, 128), F32),
        vmem((32, 128), BF16),
        vmem((NY, 32, 128), BF16),
        vmem((NY, 32, 128), BF16),
        vmem((8, 128), F32),
        vmem((NX, 8, 128), F32),
        vmem((16, 128), BF16),
        vmem((NY, 16, 128), BF16),
        vmem((NX, 144, 128), BF16),
        vmem((NX, 144, 128), BF16),
        vmem((144, 128), BF16),
        vmem((NY, 144, 128), BF16),
        vmem((NX, 2, 8, 128), F32),
        vmem((NX, 2, 8, 128), F32),
        dma((16,)),
        dma((CHUNKS + 1,)),
        dma((SLOTS,)),
        dma((1,)),
        dma((1,)),
        dma((NX,)),
        dma((NX,)),
        dma((NY,)),
        dma((NY,)),
        dma((1,)),
        dma((1,)),
        dma((NX,)),
        dma((NX,)),
        dma((NY,)),
        dma((NY,)),
        dma((NX,)),
        dma((NX,)),
        dma((NY,)),
        dma((NY,)),
        dma((NX,)),
        dma((NX,)),
    ]
    result = pl.pallas_call(
        kernel,
        out_shape=jax.ShapeDtypeStruct((1, 1024), F32),
        in_specs=[hbm] * 19,
        out_specs=pl.BlockSpec(memory_space=pltpu.VMEM),
        scratch_shapes=scratch,
        compiler_params=pltpu.CompilerParams(
            collective_id=0, has_side_effects=True, vmem_limit_bytes=56 * 1024 * 1024
        ),
        name="layer",
    )(
        tenant,
        lengths,
        hidden,
        norm_gain.reshape(128, 128),
        q_codes,
        q_absmax,
        kv_codes.T,
        kv_absmax,
        o_codes,
        o_absmax,
        down_rows(q_down),
        up_rows(q_up),
        q_magnitude,
        down_rows(o_down),
        up_rows(o_up),
        o_magnitude,
        page_table,
        kv_cache,
        jnp.asarray(constants()),
    )
    return result.astype(BF16)


def solution(mesh):
    in_specs = (
        P(),
        P(),
        P("gx", "gy"),
        P("gx", "gy"),
        P("gx", "gy"),
        P("gx", "gy"),
        P("gx", "gy"),
        P("gx", "gy"),
        P(None, "gx", None),
        P(None, None, "gy"),
        P(None, "gy"),
        P(None, "gx", None),
        P(None, None, "gy"),
        P(None, "gy"),
        P(),
        P(),
        P(),
        P(("gx", "gy"), None, None, None),
    )
    return jax.shard_map(
        local, mesh=mesh, in_specs=in_specs, out_specs=P("gx", "gy"), check_vma=False
    )
```
